256 devices in a mesh: fact: 64 (over z, y, core), feat: 4 (over x).
Axes of the slice: x: 4, y: 4, z: 8, core: 2. Of those that a mesh axis runs over, the one named last changes fastest.
Arguments:
- fact_x: bfloat16 [65536, 512], P('fact', 'feat'), may hold values from -16 to 16
- dim_owner: int32 [65536, 1], P('fact'), may hold values from 0 to 63; in each aligned block of 1024 rows (0 to 1023, 1024 to 2047, ...) at most 48 rows name the same one
- dim_slot: int32 [65536], P('fact'), may hold values from 0 to 127
- fact_owner: int32 [65536, 1], P('fact'), may hold values from 0 to 63; in each aligned block of 1024 rows (0 to 1023, 1024 to 2047, ...) at most 48 rows name the same one
- fact_slot: int32 [65536], P('fact'), may hold values from 0 to 127
- dim_table: bfloat16 [8192, 512], P('fact', 'feat'), may hold values from -6 to 6
- entity_h: bfloat16 [8192, 512], P('fact', 'feat'), may hold values from -16 to 16
- w_msg: bfloat16 [512, 512], P(None, 'feat'), may hold values from -0.25 to 0.25
- w_self: bfloat16 [512, 512], P(None, 'feat'), may hold values from -0.25 to 0.25
- w_neigh: bfloat16 [512, 512], P(None, 'feat'), may hold values from -0.25 to 0.25
- cotangent: bfloat16 [8192, 512], P('fact', 'feat'), may hold values from -0.59765625 to 0.59765625
Outputs:
- output_h: bfloat16 [8192, 512], P('fact', 'feat')
- grad_w_msg: float32 [512, 512], P('fact', 'feat')
- grad_w_self: float32 [512, 512], P('fact', 'feat')
- grad_w_neigh: float32 [512, 512], P('fact', 'feat')
- grad_dim: float32 [8192, 512], P('fact', 'feat')
The draws below stay inside these ranges and needn't reach their ends.
Inputs may be any that keep to these rules, and one draw needn't show every extreme that they name: `fact_owner`: among the fact rows of one index of fact, no key range is named by more than 48 rows, and some key range by exactly 48. `dim_owner`: among the fact rows of one index of fact, no block of the dimension table is named by more than 48 rows, and some block by exactly 48.
All inputs are finite; a program needn't handle non-finite values.
Results may differ from the reference program's by a relative error of at most 0.0059.
Values may be sent and summed in bfloat16 or wider, within the bound.
A program may use at most 64 MiB of HBM per device.

```python
import math
import jax
import jax.numpy as jnp
import numpy as np

D = 512
DIM_ROWS = 8192
F_DEV = 1024
E_DEV = 128
FACTS = 65536
ENTITIES = 8192
OWNERS = 64
CAP = 48
N_FACT = 64


def touch_ends(entries, key, smallest, high):
    longest = entries.shape.index(max(entries.shape))
    spots = []
    for shift in (0, 1):
        where = [jax.random.randint(jax.random.fold_in(key, axis), (), 0, length) for axis, length in enumerate(entries.shape)]
        where[longest] = (where[longest] + shift) % entries.shape[longest]
        spots.append(tuple(where))
    return entries.at[spots[0]].set(smallest).at[spots[1]].set(high)


def with_spikes(array, rng, source, target, blocks, factor):
    def block_of(dim):
        return (jnp.arange(array.shape[dim]) // (array.shape[dim] // blocks)).reshape((-1,) + (1,) * (array.ndim - 1 - dim))

    first = jax.random.permutation(rng, blocks)[block_of(target)]
    other_side = (block_of(target) + blocks // 2) % blocks
    return jnp.where((block_of(source) == first) | (block_of(source) == other_side), factor * array, array)


def block_levels(stream_key, extent, split, least, high):
    loudness = 1.0
    for position, parts in split:
        heights = jax.random.uniform(jax.random.fold_in(jax.random.fold_in(stream_key, 6), position), (parts,), jnp.float32, least / len(split), high / len(split))
        loudness = loudness * jnp.repeat(jnp.exp(heights), extent[position] // parts).reshape((-1,) + (1,) * (len(extent) - 1 - position))
    return loudness


def deal_out(own_key, own, number, rows, amount, top, bound, skew):
    order = jax.random.permutation(own_key, amount)
    heavy_load, common = portions_of(amount, rows * top, bound, skew, True), portions_of(amount, rows * top, bound, skew, False)
    places = jnp.arange(amount)

    def named(sizes, offset_by):
        used = int((sizes > 0).sum())
        fixed = max(1, used // 4)
        passed = fixed + (places - fixed + offset_by * (used - fixed)) % max(1, amount - fixed)
        return jnp.zeros((amount,), jnp.int32).at[order[jnp.where(places < fixed, places, passed)]].set(jnp.asarray(sizes, jnp.int32))

    sizes = jnp.where(number % 4 == 0, named(heavy_load, number // 4), named(common, number - number // 4 - 1))
    mixed = jax.random.permutation(jax.random.fold_in(own, 3), amount)
    donor, taker = mixed[0:amount // 2 * 2:2], mixed[1:amount // 2 * 2:2]
    slack = jnp.minimum(sizes[donor] - 1, bound - sizes[taker]) // 2
    slack = jnp.where((donor == order[0]) | (taker == order[0]) | (sizes[taker] == 0), 0, jnp.maximum(slack, 0))
    passed = jax.random.randint(jax.random.fold_in(own, 4), (amount // 2,), 0, 1 << 20) % (slack + 1)
    sizes = sizes.at[donor].add(-passed).at[taker].add(passed)
    items = jnp.searchsorted(jnp.cumsum(sizes), jnp.arange(rows * top), side="right").astype(jnp.int32)
    table = items.reshape(top, rows).T
    table = table[jax.random.permutation(jax.random.fold_in(own, 1), rows)]
    offset_by = jax.random.randint(jax.random.fold_in(own, 2), (rows, 1), 0, top)
    return jnp.take_along_axis(table, (jnp.arange(top)[None, :] + offset_by) % top, axis=1)


def portions_of(number_of, total, bound, lean, full):
    weights = [(1 << 20) // math.isqrt(standing ** lean) + 1 for standing in range(1, number_of + 1)]
    largest = bound if full else min(bound, max(-(-total // number_of), total * weights[0] // sum(weights)))
    least = 1 if total - largest >= number_of - 1 else 0
    holding, surplus = [largest] + [least] * (number_of - 1), total - largest - least * (number_of - 1)
    while surplus > 0:
        movable = [i for i in range(1, number_of) if holding[i] < largest] or [i for i in range(1, number_of) if holding[i] < bound]
        pool, remaining = sum([weights[i] for i in movable]), surplus
        for i in movable:
            more = min(bound - holding[i], max(1, remaining * weights[i] // pool), surplus)
            holding[i] = holding[i] + more
            surplus = surplus - more
    return np.array(holding)


def scatter_about(own_key, extent, scale, limit, split=(), kind=jnp.bfloat16):
    values = jax.random.normal(own_key, extent, jnp.float32) * scale
    if len(split) > 0:
        values = block_levels(own_key, extent, split, -0.22, 0.18) * values
    return jnp.clip(values, min=-limit, max=limit).astype(kind)


def bell_draw_with(own_key, shape, spread, reach, pieces, heavy, held_as=jnp.bfloat16):
    drawn = spread * jax.random.normal(own_key, shape, jnp.float32)
    if pieces:
        drawn = drawn * block_levels(own_key, shape, pieces, -0.22, 0.18)
    return jnp.clip(with_spikes(drawn, jax.random.fold_in(own_key, 3), *heavy), -reach, reach).astype(held_as)


def setup_inputs(seed: int = 0) -> dict:
    key_of = jax.random.split(jax.random.key(seed), 12)
    fact_x = bell_draw_with(key_of[0], (FACTS, D), 1.0, 16.0, ((0, 64), (1, 4)), (0, 1, 64, 4.0))
    dim_owner_keys = jax.random.split(jax.random.fold_in(key_of[1], 1), FACTS // F_DEV)
    dim_owner_turns = jax.random.permutation(jax.random.fold_in(key_of[1], 3), FACTS // F_DEV)
    dim_owner = jax.vmap(lambda own, number: deal_out(jax.random.fold_in(key_of[1], 2), own, number, F_DEV, OWNERS, 1, CAP, 2))(dim_owner_keys, dim_owner_turns).reshape((FACTS, 1))
    dim_slot = touch_ends(jax.random.randint(key_of[2], (FACTS,), 0, DIM_ROWS // N_FACT), jax.random.fold_in(key_of[2], 1), 0, (DIM_ROWS // N_FACT) - 1).astype(jnp.int32)
    fact_owner_keys = jax.random.split(jax.random.fold_in(key_of[3], 1), FACTS // F_DEV)
    fact_owner_turns = jax.random.permutation(jax.random.fold_in(key_of[3], 3), FACTS // F_DEV)
    fact_owner = jax.vmap(lambda own, number: deal_out(jax.random.fold_in(key_of[3], 2), own, number, F_DEV, OWNERS, 1, CAP, 2))(fact_owner_keys, fact_owner_turns).reshape((FACTS, 1))
    fact_slot = touch_ends(jax.random.randint(key_of[4], (FACTS,), 0, E_DEV), jax.random.fold_in(key_of[4], 1), 0, E_DEV - 1).astype(jnp.int32)
    dim_table = scatter_about(key_of[5], (DIM_ROWS, D), 1.0, 6.0, ((0, 64), (1, 4)))
    entity_h = bell_draw_with(key_of[6], (ENTITIES, D), 1.0, 16.0, ((0, 64), (1, 4)), (0, 1, 64, 4.0))
    w_msg = scatter_about(key_of[7], (D, D), D ** -0.5, 0.25, ((1, 4),))
    w_self = scatter_about(key_of[8], (D, D), D ** -0.5, 0.25, ((1, 4),))
    w_neigh = scatter_about(key_of[9], (D, D), D ** -0.5, 0.25, ((1, 4),))
    cotangent = scatter_about(key_of[10], (ENTITIES, D), 0.1, 0.59765625, ((0, 64), (1, 4)))
    return dict(fact_x=fact_x, dim_owner=dim_owner, dim_slot=dim_slot, fact_owner=fact_owner, fact_slot=fact_slot, dim_table=dim_table, entity_h=entity_h, w_msg=w_msg, w_self=w_self, w_neigh=w_neigh, cotangent=cotangent)


def silu_slope(values):
    sigmoid_v = jax.nn.sigmoid(values)
    return sigmoid_v * (1.0 + values * (1.0 - sigmoid_v))


def reference(fact_x, dim_owner, dim_slot, fact_owner, fact_slot, dim_table, entity_h, w_msg, w_self, w_neigh, cotangent):
    entity = (fact_owner[:, 0] * E_DEV + fact_slot).astype(jnp.int32)
    fact_dim = (dim_owner[:, 0] * (DIM_ROWS // N_FACT) + dim_slot).astype(jnp.int32)
    msg_pre = jnp.dot(fact_x, w_msg, preferred_element_type=jnp.float32) + dim_table[fact_dim].astype(jnp.float32)
    message = jax.nn.silu(msg_pre).astype(jnp.bfloat16)
    entity_sums = jax.ops.segment_sum(message.astype(jnp.float32), entity, num_segments=ENTITIES)
    counts = jax.ops.segment_sum(jnp.ones(entity.shape, jnp.float32), entity, num_segments=ENTITIES)
    divisor = jnp.maximum(counts, 1.0)
    aggregate = (entity_sums / divisor[:, None]).astype(jnp.bfloat16)
    pre_act = jnp.dot(entity_h, w_self, preferred_element_type=jnp.float32) + jnp.dot(aggregate, w_neigh, preferred_element_type=jnp.float32)
    output_h = jax.nn.silu(pre_act).astype(jnp.bfloat16)
    d_pre = (cotangent.astype(jnp.float32) * silu_slope(pre_act)).astype(jnp.bfloat16)
    grad_w_self = jnp.dot(entity_h.T, d_pre, preferred_element_type=jnp.float32)
    grad_w_neigh = jnp.dot(aggregate.T, d_pre, preferred_element_type=jnp.float32)
    d_agg = jnp.dot(d_pre, w_neigh.T, preferred_element_type=jnp.float32)
    d_scaled = (d_agg / divisor[:, None]).astype(jnp.bfloat16)
    d_msgpre = (d_scaled[entity].astype(jnp.float32) * silu_slope(msg_pre)).astype(jnp.bfloat16)
    grad_w_msg = jnp.dot(fact_x.T, d_msgpre, preferred_element_type=jnp.float32)
    grad_dim = jax.ops.segment_sum(d_msgpre.astype(jnp.float32), fact_dim, num_segments=DIM_ROWS)
    return output_h, grad_w_msg, grad_w_self, grad_w_neigh, grad_dim
```

```python
import functools

import jax
import jax.numpy as jnp
from jax import lax
from jax.experimental import pallas as pl
from jax.experimental.pallas import tpu as pltpu
from jax.sharding import PartitionSpec as P

MESH = pl.DeviceIdType.MESH
BF = jnp.bfloat16
F32 = jnp.float32

NZ, NY = 8, 4
GATHER = (0, -1, 1, -2, 2, -3, 3, -4)
REDUCE = (4, -3, 3, -2, 2, -1, 1, 0)
YD = (1, 3, 2)
ROWS = 1024
TILE = 256
W = 128
EXTRA = 160


def sigmoid_of(v):
    return 1.0 / (1.0 + jnp.exp(-v))


def kernel(
    x_ref,
    dim_own_ref,
    dim_slot_ref,
    ent_own_ref,
    ent_slot_ref,
    table_ref,
    h_ref,
    w_msg_ref,
    w_self_ref,
    w_neigh_ref,
    cot_ref,
    out_ref,
    gwm_ref,
    gws_ref,
    gwn_ref,
    gdim_ref,
    xs,
    tab,
    b_dim,
    b_ent,
    bt_dim,
    bt_ent,
    o_dim,
    o_ent,
    ot_dim,
    ot_ent,
    acc,
    dmsg,
    slope,
    val,
    ch,
    cs,
    cr1,
    cr2,
    hx,
    cx,
    ax,
    w2,
    pre,
    gw,
    pown,
    yown,
    psend1,
    precv1,
    ysend1,
    yrecv1,
    zsend1,
    zrecv1,
    psend2,
    precv2,
    ysend2,
    yrecv2,
    zsend2,
    zrecv2,
    res1,
    res2,
    div,
    s_ch,
    r_ch,
    s_y,
    r_y,
    s_p,
    r_p,
    s_ch2,
    r_ch2,
    s_y2,
    r_y2,
    s_p2,
    r_p2,
    s_x,
    r_x,
    s_h,
    r_h,
    s_c,
    r_c,
    s_w,
    r_w,
    s_wp,
    r_wp,
    s_a,
    r_a,
    s_n1,
    r_n1,
    s_n2,
    r_n2,
):
    f = lax.axis_index("fact")
    g = lax.axis_index("feat")
    z, y, c = f // 8, lax.rem(f // 2, 4), lax.rem(f, 2)
    q = lax.rem(f, 8)

    def at(zz, yy, cc):
        return (zz * 4 + yy) * 2 + cc

    zs = [lax.rem(z + d, NZ) for d in range(NZ)]
    ys = [lax.rem(y + d, NY) for d in range(NY)]
    gs = [lax.rem(g + d, 4) for d in range(4)]
    right, left, mate = at(zs[1], y, c), at(zs[7], y, c), at(z, y, 1 - c)
    zpeer = [at(zs[d], y, c) for d in range(NZ)]
    ypeer = [at(z, ys[d], c) for d in YD]
    qpeer = [z * 8 + lax.rem(q + d, 8) for d in range(8)]

    def remote(src, dst, ssem, rsem, to_f, to_g=None):
        return pltpu.make_async_remote_copy(
            src_ref=src,
            dst_ref=dst,
            send_sem=ssem,
            recv_sem=rsem,
            device_id=(to_f, g if to_g is None else to_g),
            device_id_type=MESH,
        )

    even, odd = c == 0, c == 1

    barrier = pltpu.get_barrier_semaphore()
    friends = [(p, g) for p in zpeer[1:]] + [(p, g) for p in qpeer[1:]] + [(f, p) for p in gs[1:]]
    for friend in friends:
        pl.semaphore_signal(barrier, inc=1, device_id=friend, device_id_type=MESH)
    pl.semaphore_wait(barrier, len(friends))

    half = [pl.ds(0, ROWS // 2), pl.ds(ROWS // 2, ROWS // 2)]

    def x_copy(n):
        if n < 4:
            to, part = ((1, 0), (3, 1), (1, 1), (3, 0))[n]
            src, dst = x_ref.at[half[part]], xs.at[g, half[part]]
        elif n == 4:
            to, src = 1, xs.at[gs[3], half[0]]
            dst = src
        else:
            to, src = 3, xs.at[gs[1], half[1]]
            dst = src
        return remote(src, dst, s_x.at[n], r_x.at[n], f, gs[to])

    def x_landed(n):
        block, part = ((3, 0), (1, 1), (3, 1), (1, 0), (2, 0), (2, 1))[n]
        dst = xs.at[gs[block], half[part]]
        remote(dst, dst, s_x.at[n], r_x.at[n], f, gs[1]).wait_recv()

    def gather_sends(k):
        zk = zs[GATHER[k] % NZ]
        both = {}
        for parity in (0, 1):
            unit = tab.at[0, zk] if parity == 0 else tab.at[1, zk, y]
            group = tab.at[parity, zk]
            chain = []
            if -4 < GATHER[k] <= 0:
                chain.append((unit, s_ch.at[k], r_ch.at[k + 2 if k else 1], right))
            if 0 <= GATHER[k] < 3:
                chain.append((unit, s_ch.at[k if k else 8], r_ch.at[k + 2], left))
            spread = []
            if parity == 1:
                spread = [
                    (unit, s_y.at[k, i], r_y.at[k, i], ypeer[i]) for i in range(3)
                ]
            both[parity] = (chain, spread, (group, s_p.at[k], r_p.at[k], mate))
        return both

    def first_spread():
        unit = tab.at[0, z, y]
        return [(unit, s_y.at[0, i], r_y.at[0, i], ypeer[i]) for i in range(3)]

    def go(item):
        unit, ssem, rsem, to = item
        remote(unit, unit, ssem, rsem, to).start()

    def landed(dst, ssem, rsem):
        remote(dst, dst, ssem, rsem, mate).wait_recv()

    def gather_open(own):
        @pl.when(even)
        def _():
            tab[0, z, y] = own
            for item in first_spread():
                go(item)

        @pl.when(odd)
        def _():
            tab[1, z, y] = own

    def gather_comm1(k):
        zk = zs[GATHER[k] % NZ]
        sends = gather_sends(k)

        @pl.when(even)
        def _():
            if k == 0:
                for i, d in enumerate(YD):
                    landed(tab.at[0, z, ys[(NY - d) % NY]], s_y.at[0, i], r_y.at[0, i])
            else:
                landed(tab.at[0, zk], s_ch.at[k], r_ch.at[k])
            chain, _, group = sends[0]
            for item in chain:
                go(item)
            go(group)

        @pl.when(odd)
        def _():
            if k > 0:
                landed(tab.at[1, zk, y], s_ch.at[k], r_ch.at[k])
            chain, spread, _ = sends[1]
            for item in chain + spread:
                go(item)

    def gather_comm2(k):
        zk = zs[GATHER[k] % NZ]
        sends = gather_sends(k)

        @pl.when(odd)
        def _():
            for i, d in enumerate(YD):
                landed(tab.at[1, zk, ys[(NY - d) % NY]], s_y.at[k, i], r_y.at[k, i])
            go(sends[1][2])

    def gather_wait(k):
        landed(tab.at[1 - c, zs[GATHER[k] % NZ]], s_p.at[k], r_p.at[k])

    def gather_drain():
        for parity, mine in ((0, even), (1, odd)):

            @pl.when(mine)
            def _():
                items = first_spread() if parity == 0 else []
                for k in range(8):
                    chain, spread, group = gather_sends(k)[parity]
                    items += chain + spread + [group]
                for unit, ssem, rsem, to in items:
                    remote(unit, unit, ssem, rsem, to).wait_send()

    def pick(k, owners, slots, into):
        zk = zs[GATHER[k] % NZ]
        base = (zk * 8).astype(F32)

        def tile(t, carry):
            rows = pl.ds(pl.multiple_of(t * TILE, TILE), TILE)
            rel = owners[rows, :] - jnp.full((TILE, W), base, F32).astype(BF)
            ones = slots[rows, :]
            parts = []
            for parity in (0, 1):
                for yy in range(NY):
                    wanted = jnp.asarray(yy * 2 + parity, BF)
                    parts.append(jnp.where(rel == wanted, ones, jnp.zeros_like(ones)))
            lhs = jnp.concatenate(parts, axis=1)
            rhs = jnp.concatenate(
                [tab[0, zk].reshape(NY * W, W), tab[1, zk].reshape(NY * W, W)], axis=0
            )
            got = jnp.dot(lhs, rhs, preferred_element_type=F32)
            if k == 0:
                into[rows, :] = got
            else:
                into[rows, :] += got
            return carry

        lax.fori_loop(0, ROWS // TILE, tile, 0)

    def lane_rows(index_ref, i):
        return jnp.broadcast_to(index_ref[i : i + 1, :].astype(F32), (W, W))

    sub = lax.broadcasted_iota(jnp.int32, (W, W), 0)
    lane = lax.broadcasted_iota(jnp.int32, (W, W), 1)
    eye = sub == lane
    subf, lanef = sub.astype(F32), lane.astype(F32)
    ones_w = jnp.ones((W, W), BF)

    def prepare(own_ref, slot_ref, slots, slots_t, owners, owners_t):
        for i in range(ROWS // W):
            span = slice(i * W, (i + 1) * W)
            srow, orow = lane_rows(slot_ref, i), lane_rows(own_ref, i)
            slots_t[:, span] = jnp.where(srow == subf, 1.0, 0.0).astype(BF)
            scol = jnp.dot(
                jnp.where(eye, srow, 0.0).astype(BF), ones_w, preferred_element_type=F32
            )
            slots[span, :] = jnp.where(scol == lanef, 1.0, 0.0).astype(BF)
            ocol = jnp.dot(
                jnp.where(eye, orow, 0.0).astype(BF), ones_w, preferred_element_type=F32
            )
            owners[span, :] = ocol.astype(BF)
            oint = own_ref[i : i + 1, :]
            parity = lax.rem(oint, 2)
            flipped = oint + c * (1 - 2 * parity)
            owners_t[:, span] = jnp.broadcast_to(flipped.astype(F32), (W, W)).astype(BF)

    def reduce_next(j):
        d = REDUCE[j]
        if d > 0:
            return right, (j + 2 if j + 2 < 8 else 7)
        return left, (j + 2 if j + 2 < 7 else 8)

    def reduce_block(j, source, psend, grads):
        tz = zs[REDUCE[j] % NZ]
        owners_t, slots_t = (ot_dim, bt_dim) if grads else (ot_ent, bt_ent)

        def block(yy, carry):
            base = (tz * 8 + yy * 2).astype(F32)
            rel = owners_t[...] - jnp.full((W, ROWS), base, F32).astype(BF)
            ones = slots_t[...]
            zero = jnp.zeros_like(ones)
            lhs = jnp.concatenate(
                [
                    jnp.where(rel == jnp.asarray(0, BF), ones, zero),
                    jnp.where(rel == jnp.asarray(1, BF), ones, zero),
                ],
                axis=0,
            )
            got = jnp.dot(lhs, source[...], preferred_element_type=F32)
            pown[j, yy, 0:W] = got[0:W]
            psend[j, yy, 0:W] = got[W : 2 * W].astype(BF)
            if grads:
                first = tz * 8 + yy * 2
                mine = pl.ds(pl.multiple_of((first + c) * 8, 8), 8)
                other = pl.ds(pl.multiple_of((first + 1 - c) * 8, 8), 8)
                blank = jnp.zeros((8, W), F32)
                for n in range(3):
                    pown[j, yy, W + 8 * n : W + 8 * n + 8] = gw[n, mine, :]
                pown[j, yy, W + 24 : W + 32] = blank
                psend[j, yy, W : W + 16] = jnp.concatenate(
                    [gw[0, other, :], gw[1, other, :]], axis=0
                ).astype(BF)
                psend[j, yy, W + 16 : W + 32] = jnp.concatenate(
                    [gw[2, other, :], blank], axis=0
                ).astype(BF)
            return carry

        lax.fori_loop(0, NY, block, 0)

    def reduce_all(source, psend, precv, ysend, yrecv, zsend, zrecv, res, grads):
        tall = pl.ds(0, EXTRA if grads else W)

        def to_mate(j):
            return remote(psend.at[j], precv.at[j], s_p2.at[j], r_p2.at[j], mate)

        def to_next(j, parity):
            to, slot = reduce_next(j)
            src, dst = zsend.at[j], zrecv.at[slot]
            if parity:
                src, dst = zsend.at[j, 0], zrecv.at[slot, 0]
            return remote(src, dst, s_ch2.at[j], r_ch2.at[slot], to)

        def to_y(j, i):
            return remote(ysend.at[j, i], yrecv.at[j, i], s_y2.at[j, i], r_y2.at[j, i], ypeer[i])

        def from_chain(j, parity):
            slots = [] if j < 2 else ([j] if j < 7 else [7, 8])
            total = None
            for slot in slots:
                dst = zrecv.at[slot, 0] if parity else zrecv.at[slot]
                landed(dst, s_ch2.at[0], r_ch2.at[slot])
                piece = dst[...].astype(F32)
                total = piece if total is None else total + piece
            return total

        def from_y(j):
            total = yown[j, tall]
            for i in range(3):
                landed(yrecv.at[j, i], s_y2.at[j, i], r_y2.at[j, i])
            for i in range(3):
                total = total + yrecv[j, i].astype(F32)
            return total

        def stage1(j):
            landed(precv.at[j], s_p2.at[j], r_p2.at[j])
            pown[j, :, tall] = pown[j, :, tall] + precv[j].astype(F32)

            @pl.when(even)
            def _():
                chain = from_chain(j, 0)
                total = pown[j, :, tall]
                if chain is not None:
                    total = total + chain
                if j < 7:
                    zsend[j] = total.astype(BF)
                    to_next(j, 0).start()
                else:
                    pown[j, :, tall] = total
                    spread_y(j)

            @pl.when(odd)
            def _():
                spread_y(j)

        def spread_y(j):
            for i, d in enumerate(YD):
                ysend[j, i] = pown[j, ys[d], tall].astype(BF)
                to_y(j, i).start()
            yown[j, tall] = pown[j, y, tall]

        def stage2(j):
            @pl.when(odd)
            def _():
                total = from_y(j)
                chain = from_chain(j, 1)
                if chain is not None:
                    total = total + chain
                if j < 7:
                    zsend[j, 0] = total.astype(BF)
                    to_next(j, 1).start()
                else:
                    res[...] = total

            if j == 7:

                @pl.when(even)
                def _():
                    res[...] = from_y(7)

        for step in range(10):
            if step < 8:
                reduce_block(step, source, psend, grads)
                to_mate(step).start()
            if 1 <= step < 9:
                stage1(step - 1)
            if step >= 2:
                stage2(step - 2)

        def drain():
            for j in range(8):
                to_mate(j).wait_send()

            @pl.when(even)
            def _():
                for j in range(7):
                    to_next(j, 0).wait_send()
                for i in range(3):
                    to_y(7, i).wait_send()

            @pl.when(odd)
            def _():
                for j in range(7):
                    to_next(j, 1).wait_send()
                for j in range(8):
                    for i in range(3):
                        to_y(j, i).wait_send()

        return drain

    def small(src, dst, ssem, rsem, i):
        return remote(src, dst, ssem.at[i], rsem.at[i], f, gs[YD[i]])

    def small_landed(dst, ssem, rsem):
        for i, d in enumerate(YD):
            ref = dst(gs[(4 - d) % 4])
            remote(ref, ref, ssem.at[i], rsem.at[i], f, gs[1]).wait_recv()

    def h_copy(i):
        return small(h_ref, hx.at[g], s_h, r_h, i)

    def c_copy(i):
        return small(cot_ref, cx.at[g], s_c, r_c, i)

    def w_copy(i):
        return small(w2.at[c, g], w2.at[c, g], s_w, r_w, i)

    def w_mate(i):
        unit = w2.at[c, gs[(4 - YD[i]) % 4]]
        return remote(unit, unit, s_wp.at[i], r_wp.at[i], mate)

    def a_copy(i):
        return small(ax.at[g], ax.at[g], s_a, r_a, i)

    def n1_copy(d):
        return remote(ch.at[zs[d]], cr1.at[d - 1], s_n1.at[d - 1], r_n1.at[d - 1], zpeer[d])

    def n2_copy(d):
        return remote(cs, cr2.at[d - 1], s_n2.at[d - 1], r_n2.at[d - 1], qpeer[d])

    gather_open(table_ref[...])
    for n in range(4):
        x_copy(n).start()
    gather_comm1(0)
    prepare(dim_own_ref, dim_slot_ref, b_dim, bt_dim, o_dim, ot_dim)
    xs[g] = x_ref[...]
    hx[g] = h_ref[...]
    cx[g] = cot_ref[...]
    w2[0, g] = w_self_ref[...]
    w2[1, g] = w_neigh_ref[...]
    gather_comm1(1)
    gather_comm2(0)
    prepare(ent_own_ref, ent_slot_ref, b_ent, bt_ent, o_ent, ot_ent)

    owner_no = lax.broadcasted_iota(jnp.int32, (64, W), 0).astype(F32)
    hits = jnp.zeros((64, W), F32)
    for i in range(ROWS // W):
        orow = jnp.broadcast_to(ent_own_ref[i : i + 1, :].astype(F32), (64, W))
        named = jnp.where(orow == owner_no, 1.0, 0.0).astype(BF)
        hits = hits + jnp.dot(named, b_ent[i * W : (i + 1) * W, :], preferred_element_type=F32)
    ch[...] = hits.reshape(8, 8, W)
    for d in range(1, 8):
        n1_copy(d).start()

    for step in range(2, 10):
        if step < 8:
            gather_comm1(step)
        if step - 1 < 8:
            gather_comm2(step - 1)
        if step == 5:
            x_landed(0)
            x_copy(4).start()
            x_landed(1)
            x_copy(5).start()
        gather_wait(step - 2)
        pick(step - 2, o_dim, b_dim, acc)

    for n in range(2, 6):
        x_landed(n)
    for i in range(3):
        h_copy(i).start()
        c_copy(i).start()
        w_copy(i).start()

    def message_tile(t, carry):
        rows = pl.ds(pl.multiple_of(t * TILE, TILE), TILE)
        feats = jnp.concatenate([xs[b, rows, :] for b in range(4)], axis=1)
        v = acc[rows, :] + jnp.dot(feats, w_msg_ref[...], preferred_element_type=F32)
        s = sigmoid_of(v)
        val[rows, :] = (v * s).astype(BF)
        slope[rows, :] = s * (1.0 + v * (1.0 - s))
        return carry

    lax.fori_loop(0, ROWS // TILE, message_tile, 0)
    gather_drain()

    for d in range(1, 8):
        ref = cr1.at[d - 1]
        landed(ref, s_n1.at[d - 1], r_n1.at[d - 1])
    zsum = ch[z]
    for d in range(1, 8):
        zsum = zsum + cr1[d - 1]
    cs[...] = zsum
    for d in range(1, 8):
        n2_copy(d).start()

    drain1 = reduce_all(val, psend1, precv1, ysend1, yrecv1, zsend1, zrecv1, res1, False)

    for d in range(1, 8):
        landed(cr2.at[d - 1], s_n2.at[d - 1], r_n2.at[d - 1])
    hsum = cs[...]
    for d in range(1, 8):
        hsum = hsum + cr2[d - 1]
    row_no = lax.broadcasted_iota(jnp.int32, (8, W), 0)
    mine_row = jnp.sum(jnp.where(row_no == q, hsum, 0.0), axis=0, keepdims=True)
    column = jnp.sum(
        jnp.where(eye, jnp.broadcast_to(mine_row, (W, W)), 0.0), axis=1, keepdims=True
    )
    div[...] = jnp.broadcast_to(jnp.maximum(column, 1.0), (W, W))

    ax[g] = (res1[...] / div[...]).astype(BF)
    for i in range(3):
        a_copy(i).start()
    drain1()
    small_landed(lambda b: hx.at[b], s_h, r_h)
    small_landed(lambda b: cx.at[b], s_c, r_c)
    small_landed(lambda b: w2.at[c, b], s_w, r_w)
    for i in range(3):
        w_mate(i).start()
    h_full = jnp.concatenate([hx[b] for b in range(4)], axis=1)
    for i, d in enumerate(YD):
        ref = w2.at[1 - c, gs[(4 - d) % 4]]
        landed(ref, s_wp.at[i], r_wp.at[i])
    for b in range(4):
        pre[b] = jnp.dot(h_full, w2[0, b], preferred_element_type=F32)
    small_landed(lambda b: ax.at[b], s_a, r_a)
    a_full = jnp.concatenate([ax[b] for b in range(4)], axis=1)
    d_agg = jnp.zeros((W, W), F32)
    mine_rows = pl.ds(pl.multiple_of(g * W, W), W)
    for b in range(4):
        v = pre[b] + jnp.dot(a_full, w2[1, b], preferred_element_type=F32)
        pre[b] = v
        s = sigmoid_of(v)
        d_pre = (cx[b].astype(F32) * (s * (1.0 + v * (1.0 - s)))).astype(BF)
        d_agg = d_agg + lax.dot_general(
            d_pre, w2[1, b, mine_rows, :], (((1,), (1,)), ((), ())), preferred_element_type=F32
        )
    gather_open((d_agg / div[...]).astype(BF))
    gather_comm1(0)
    v = pre[g]
    s = sigmoid_of(v)
    out_ref[...] = (v * s).astype(BF)
    d_pre = (cot_ref[...].astype(F32) * (s * (1.0 + v * (1.0 - s)))).astype(BF)
    for b in range(4):
        span = slice(b * W, (b + 1) * W)
        gw[1, span, :] = lax.dot_general(
            hx[b], d_pre, (((0,), (0,)), ((), ())), preferred_element_type=F32
        )
        gw[2, span, :] = lax.dot_general(
            ax[b], d_pre, (((0,), (0,)), ((), ())), preferred_element_type=F32
        )

    for step in range(1, 10):
        if step < 8:
            gather_comm1(step)
        if 0 <= step - 1 < 8:
            gather_comm2(step - 1)
        if step >= 2:
            gather_wait(step - 2)
            pick(step - 2, o_ent, b_ent, dmsg)

    def back_tile(t, carry):
        rows = pl.ds(pl.multiple_of(t * TILE, TILE), TILE)
        val[rows, :] = (dmsg[rows, :] * slope[rows, :]).astype(BF)
        return carry

    lax.fori_loop(0, ROWS // TILE, back_tile, 0)
    gather_drain()
    for b in range(4):
        gw[0, b * W : (b + 1) * W, :] = lax.dot_general(
            xs[b], val[...], (((0,), (0,)), ((), ())), preferred_element_type=F32
        )
    drain2 = reduce_all(val, psend2, precv2, ysend2, yrecv2, zsend2, zrecv2, res2, True)
    gdim_ref[...] = res2[0:W]
    gwm_ref[...] = res2[W : W + 8]
    gws_ref[...] = res2[W + 8 : W + 16]
    gwn_ref[...] = res2[W + 16 : W + 24]

    drain2()
    for n in range(6):
        x_copy(n).wait_send()
    for i in range(3):
        h_copy(i).wait_send()
        c_copy(i).wait_send()
        w_copy(i).wait_send()
        w_mate(i).wait_send()
        a_copy(i).wait_send()
    for d in range(1, 8):
        n1_copy(d).wait_send()
        n2_copy(d).wait_send()


def shards(x, dim_owner, dim_slot, fact_owner, fact_slot, table, h, w_msg, w_self, w_neigh, cot):
    tile = (ROWS // W, W)
    vmem = pl.BlockSpec(memory_space=pltpu.VMEM)
    dma = pltpu.SemaphoreType.DMA

    def lots(tall, *lead):
        return pltpu.VMEM((*lead, tall, W), BF)

    def stages(tall):
        return [
            lots(tall, 8, NY),
            lots(tall, 8, NY),
            lots(tall, 8, 3),
            lots(tall, 8, 3),
            lots(tall, 8, NY),
            lots(tall, 9, NY),
        ]

    def sems(*shape):
        return [dma(shape), dma(shape)]

    scratch = [
        lots(ROWS, 4),
        lots(W, 2, NZ, NY),
        pltpu.VMEM((ROWS, W), BF),
        pltpu.VMEM((ROWS, W), BF),
        pltpu.VMEM((W, ROWS), BF),
        pltpu.VMEM((W, ROWS), BF),
        pltpu.VMEM((ROWS, W), BF),
        pltpu.VMEM((ROWS, W), BF),
        pltpu.VMEM((W, ROWS), BF),
        pltpu.VMEM((W, ROWS), BF),
        pltpu.VMEM((ROWS, W), F32),
        pltpu.VMEM((ROWS, W), F32),
        pltpu.VMEM((ROWS, W), F32),
        pltpu.VMEM((ROWS, W), BF),
        pltpu.VMEM((8, 8, W), F32),
        pltpu.VMEM((8, W), F32),
        pltpu.VMEM((7, 8, W), F32),
        pltpu.VMEM((7, 8, W), F32),
        lots(W, 4),
        lots(W, 4),
        lots(W, 4),
        lots(512, 2, 4),
        pltpu.VMEM((4, W, W), F32),
        pltpu.VMEM((3, 512, W), F32),
        pltpu.VMEM((8, NY, EXTRA, W), F32),
        pltpu.VMEM((8, EXTRA, W), F32),
        *stages(W),
        *stages(EXTRA),
        pltpu.VMEM((W, W), F32),
        pltpu.VMEM((EXTRA, W), F32),
        pltpu.VMEM((W, W), F32),
        *sems(9),
        *sems(8, 3),
        *sems(8),
        *sems(9),
        *sems(8, 3),
        *sems(8),
        *sems(6),
        *sems(3),
        *sems(3),
        *sems(3),
        *sems(3),
        *sems(3),
        *sems(7),
        *sems(7),
    ]
    return pl.pallas_call(
        kernel,
        out_shape=(
            jax.ShapeDtypeStruct((W, W), BF),
            jax.ShapeDtypeStruct((8, W), F32),
            jax.ShapeDtypeStruct((8, W), F32),
            jax.ShapeDtypeStruct((8, W), F32),
            jax.ShapeDtypeStruct((W, W), F32),
        ),
        in_specs=[vmem] * 11,
        out_specs=(vmem,) * 5,
        scratch_shapes=scratch,
        compiler_params=pltpu.CompilerParams(
            collective_id=0, has_side_effects=True, vmem_limit_bytes=56 * 1024 * 1024
        ),
    )(
        x,
        dim_owner.reshape(tile),
        dim_slot.reshape(tile),
        fact_owner.reshape(tile),
        fact_slot.reshape(tile),
        table,
        h,
        w_msg,
        w_self,
        w_neigh,
        cot,
    )


def solution(mesh):
    placed = (
        P("fact", "feat"),
        P("fact", None),
        P("fact"),
        P("fact", None),
        P("fact"),
        P("fact", "feat"),
        P("fact", "feat"),
        P(None, "feat"),
        P(None, "feat"),
        P(None, "feat"),
        P("fact", "feat"),
    )
    return jax.shard_map(
        shards,
        mesh=mesh,
        in_specs=placed,
        out_specs=(P("fact", "feat"),) * 5,
        check_vma=False,
    )
```

```python
import jax
import jax.numpy as jnp
from jax import lax
from jax.experimental import pallas as pl
from jax.experimental.pallas import tpu as pltpu
from jax.sharding import PartitionSpec as P

MESH = pl.DeviceIdType.MESH
BF = jnp.bfloat16
F32 = jnp.float32

NZ, NY = 8, 4
EVENTS = (0, -2, 2, -3, 3, 4, -1, 1)
FAR = 6
TARGETS = (4, -3, 1, -1, 3, -2, 2, 0)
NEAR_AT = (2, 3)
FAR_AT = (0, 1, 4, 5, 6)
YD = (1, 3, 2)
ROWS = 1024
TILE = 256
W = 128
EXTRA = 160
LAG = 5


def sigmoid_of(v):
    return 1.0 / (1.0 + jnp.exp(-v))


def kernel(
    x_ref,
    dim_own_ref,
    dim_slot_ref,
    ent_own_ref,
    ent_slot_ref,
    table_ref,
    h_ref,
    w_msg_ref,
    w_self_ref,
    w_neigh_ref,
    cot_ref,
    out_ref,
    sums_ref,
    xs,
    tab,
    b_ent,
    bt_dim,
    bt_ent,
    ot_dim,
    ot_ent,
    acc,
    slope,
    val,
    ch,
    cs,
    cr1,
    cr2,
    hx,
    cx,
    ax,
    w2,
    wm,
    pre,
    gw,
    pown,
    yown,
    psend1,
    precv1,
    gsend1,
    grecv1,
    ysend1,
    yrecv1,
    zsend1,
    zrecv1,
    psend2,
    precv2,
    gsend2,
    grecv2,
    ysend2,
    yrecv2,
    zsend2,
    zrecv2,
    res1,
    res2,
    div,
    s_ch,
    r_ch,
    s_y,
    r_y,
    s_p,
    r_p,
    s_ch2,
    r_ch2,
    s_y2,
    r_y2,
    s_p2,
    r_p2,
    s_x,
    r_x,
    s_h,
    r_h,
    s_c,
    r_c,
    s_w,
    r_w,
    s_wp,
    r_wp,
    s_a,
    r_a,
    s_n1,
    r_n1,
    s_n2,
    r_n2,
    s_in,
    keys_v,
    keys_dim,
    keys_ent,
    wide,
):
    f = lax.axis_index("fact")
    g = lax.axis_index("feat")
    z, y, c = f // 8, lax.rem(f // 2, 4), lax.rem(f, 2)
    q = lax.rem(f, 8)

    def at(zz, yy, cc):
        return (zz * 4 + yy) * 2 + cc

    zs = [lax.rem(z + d, NZ) for d in range(NZ)]
    ys = [lax.rem(y + d, NY) for d in range(NY)]
    gs = [lax.rem(g + d, 4) for d in range(4)]
    right, left, mate = at(zs[1], y, c), at(zs[7], y, c), at(z, y, 1 - c)
    zpeer = [at(zs[d], y, c) for d in range(NZ)]
    ypeer = [at(z, ys[d], c) for d in YD]
    qpeer = [z * 8 + lax.rem(q + d, 8) for d in range(8)]

    def remote(src, dst, ssem, rsem, to_f, to_g=None):
        return pltpu.make_async_remote_copy(
            src_ref=src,
            dst_ref=dst,
            send_sem=ssem,
            recv_sem=rsem,
            device_id=(to_f, g if to_g is None else to_g),
            device_id_type=MESH,
        )

    barrier = pltpu.get_barrier_semaphore()
    friends = [(p, g) for p in zpeer[1:]] + [(p, g) for p in qpeer[1:]] + [(f, p) for p in gs[1:]]
    for friend in friends:
        pl.semaphore_signal(barrier, inc=1, device_id=friend, device_id_type=MESH)

    half = [pl.ds(0, ROWS // 2), pl.ds(ROWS // 2, ROWS // 2)]

    def x_copy(n):
        if n < 4:
            to, part = ((1, 0), (3, 1), (1, 1), (3, 0))[n]
            src = xs.at[g, half[part]]
            dst = src
        elif n == 4:
            to, src = 1, xs.at[gs[3], half[0]]
            dst = src
        else:
            to, src = 3, xs.at[gs[1], half[1]]
            dst = src
        return remote(src, dst, s_x.at[n], r_x.at[n], f, gs[to])

    def x_landed(n):
        block, part = ((3, 0), (1, 1), (3, 1), (1, 0), (2, 0), (2, 1))[n]
        dst = xs.at[gs[block], half[part]]
        remote(dst, dst, s_x.at[n], r_x.at[n], f, gs[1]).wait_recv()

    def unit(k):
        return tab.at[c, zs[EVENTS[k] % NZ], y]

    def group(k):
        return tab.at[c, zs[EVENTS[k] % NZ]]

    def z_send(k):
        piece = unit(0) if k < FAR else group(0)
        return remote(piece, piece, s_ch.at[k], r_ch.at[k], zpeer[-EVENTS[k] % NZ])

    def y_send(k, i):
        return remote(unit(k), unit(k), s_y.at[k, i], r_y.at[k, i], ypeer[i])

    def p_send(k):
        return remote(group(k), group(k), s_p.at[k], r_p.at[k], mate)

    def landed(dst, ssem, rsem):
        remote(dst, dst, ssem, rsem, mate).wait_recv()

    def gather_open():
        for k in range(1, FAR):
            z_send(k).start()
        for i in range(3):
            y_send(0, i).start()

    def gather_near():
        gather_join(0)
        for k in (6, 7):
            z_send(k).start()

    def gather_spread(k):
        landed(unit(k), s_ch.at[k], r_ch.at[k])
        for i in range(3):
            y_send(k, i).start()

    def gather_join(k):
        zk = zs[EVENTS[k] % NZ]
        if k < FAR:
            for i, d in enumerate(YD):
                landed(tab.at[c, zk, ys[(NY - d) % NY]], s_y.at[k, i], r_y.at[k, i])
        else:
            landed(group(k), s_ch.at[k], r_ch.at[k])
        p_send(k).start()

    def gather_drain():
        for k in range(8):
            if k > 0:
                z_send(k).wait_send()
            if k < FAR:
                for i in range(3):
                    y_send(k, i).wait_send()
            p_send(k).wait_send()

    def gather_run(keys, sink, hooks):
        def use(k):
            zk = zs[EVENTS[k] % NZ]
            landed(tab.at[1 - c, zk], s_p.at[k], r_p.at[k])
            for parity in (0, 1):
                first = parity * NZ * NY * W + zk * (NY * W)
                rows = pl.ds(pl.multiple_of(first, NY * W), NY * W)
                wide[rows, :] = tab[parity, zk].reshape(NY * W, W).astype(F32)

        plan = (
            (gather_spread, 1),
            (gather_spread, 2),
            (use, 0),
            (gather_spread, 3),
            (gather_spread, 4),
            (gather_spread, 5),
            (gather_join, 1),
            (gather_join, 2),
            (gather_join, 6),
            (gather_join, 7),
            (gather_join, 3),
            (gather_join, 4),
            (use, 1),
            (use, 2),
            (use, 6),
            (use, 7),
            (gather_join, 5),
            (use, 3),
            (use, 4),
            (use, 5),
        )
        for n, (stage, k) in enumerate(plan):
            if n in hooks:
                hooks[n]()
            stage(k)

        def some(t, carry):
            i, first = t // 4, lax.rem(t, 4) * 32
            found = [wide[pl.ds(keys[i, first + j], 1), :] for j in range(32)]
            sink(pl.ds(pl.multiple_of(t * 32, 32), 32), jnp.concatenate(found, axis=0))
            return carry

        lax.fori_loop(0, ROWS // 32, some, 0)

    def key_tile(own_ref, slot_ref):
        owns = own_ref[...]
        return lax.rem(owns, 2) * (NZ * NY * W) + (owns // 2) * W + slot_ref[...]

    def lane_rows(index_ref, i):
        return jnp.broadcast_to(index_ref[i : i + 1, :].astype(F32), (W, W))

    sub = lax.broadcasted_iota(jnp.int32, (W, W), 0)
    lane = lax.broadcasted_iota(jnp.int32, (W, W), 1)
    eye = sub == lane
    subf, lanef = sub.astype(F32), lane.astype(F32)
    ones_w = jnp.ones((W, W), BF)

    def prepare(own_ref, slot_ref, slots, slots_t, owners_t):
        for i in range(ROWS // W):
            span = slice(i * W, (i + 1) * W)
            srow = lane_rows(slot_ref, i)
            slots_t[:, span] = jnp.where(srow == subf, 1.0, 0.0).astype(BF)
            if slots is not None:
                scol = jnp.dot(
                    jnp.where(eye, srow, 0.0).astype(BF), ones_w, preferred_element_type=F32
                )
                slots[span, :] = jnp.where(scol == lanef, 1.0, 0.0).astype(BF)
            oint = own_ref[i : i + 1, :]
            flipped = oint + c * (1 - 2 * lax.rem(oint, 2))
            owners_t[:, span] = jnp.broadcast_to(flipped.astype(F32), (W, W)).astype(BF)

    def reduce_block(j, source, psend, grads):
        tz = zs[TARGETS[j] % NZ]
        owners_t, slots_t = (ot_dim, bt_dim) if grads else (ot_ent, bt_ent)

        base = (tz * 8).astype(F32)
        rel = owners_t[...] - jnp.full((W, ROWS), base, F32).astype(BF)
        ones = slots_t[...]
        zero = jnp.zeros_like(ones)
        lhs = jnp.concatenate(
            [
                jnp.where(rel == jnp.asarray(yy * 2 + side, BF), ones, zero)
                for side in (1, 0)
                for yy in range(NY)
            ],
            axis=0,
        )
        got = jnp.dot(lhs, source[...], preferred_element_type=F32)
        for yy in range(NY):
            psend[j, yy, 0:W] = got[yy * W : (yy + 1) * W].astype(BF)
            pown[j, yy, 0:W] = got[(NY + yy) * W : (NY + yy + 1) * W]
        if grads:
            blank = jnp.zeros((8, W), F32)
            for yy in range(NY):
                first = tz * 8 + yy * 2
                mine = pl.ds(pl.multiple_of((first + c) * 8, 8), 8)
                other = pl.ds(pl.multiple_of((first + 1 - c) * 8, 8), 8)
                for n in range(3):
                    pown[j, yy, W + 8 * n : W + 8 * n + 8] = gw[n, mine, :]
                pown[j, yy, W + 24 : W + 32] = blank
                psend[j, yy, W : W + 16] = jnp.concatenate(
                    [gw[0, other, :], gw[1, other, :]], axis=0
                ).astype(BF)
                psend[j, yy, W + 16 : W + 32] = jnp.concatenate(
                    [gw[2, other, :], blank], axis=0
                ).astype(BF)

    def reduce_all(
        source, psend, precv, gsend, grecv, ysend, yrecv, zsend, zrecv, res, grads, hooks
    ):
        tall = pl.ds(0, EXTRA if grads else W)

        def to_mate(j):
            return remote(psend.at[j], precv.at[j], s_p2.at[j], r_p2.at[j], mate)

        def slot(j):
            return 5 if j == 7 else FAR_AT.index(j)

        def to_y(j, i):
            n = slot(j)
            return remote(ysend.at[n, i], yrecv.at[n, i], s_y2.at[n, i], r_y2.at[n, i], ypeer[i])

        def to_z(j):
            to = zpeer[TARGETS[j] % NZ]
            if j in NEAR_AT:
                n = NEAR_AT.index(j)
                return remote(gsend.at[n], grecv.at[n], s_ch2.at[j], r_ch2.at[j], to)
            n = slot(j)
            return remote(zsend.at[n], zrecv.at[n], s_ch2.at[j], r_ch2.at[j], to)

        def stage1(j):
            landed(precv.at[j], s_p2.at[j], r_p2.at[j])
            if j in NEAR_AT:
                gsend[NEAR_AT.index(j)] = (pown[j, :, tall] + precv[j].astype(F32)).astype(BF)
                to_z(j).start()
                return
            if j == 7:
                for n in range(2):
                    landed(grecv.at[n], s_ch2.at[NEAR_AT[n]], r_ch2.at[NEAR_AT[n]])

            def block(yy):
                got = pown[j, yy, tall] + precv[j, yy].astype(F32)
                if j == 7:
                    for n in range(2):
                        got = got + grecv[n, yy].astype(F32)
                return got

            for i, d in enumerate(YD):
                ysend[slot(j), i] = block(ys[d]).astype(BF)
                to_y(j, i).start()
            yown[j, tall] = block(y)

        def stage2(j):
            for i in range(3):
                n = slot(j)
                landed(yrecv.at[n, i], s_y2.at[n, i], r_y2.at[n, i])
            total = yown[j, tall]
            for i in range(3):
                total = total + yrecv[slot(j), i].astype(F32)
            if j < 7:
                zsend[slot(j)] = total.astype(BF)
                to_z(j).start()
            else:
                res[...] = total

        for step in range(8 + LAG):
            if step < 8:
                reduce_block(step, source, psend, grads)
                to_mate(step).start()
            if 1 <= step < 9:
                stage1(step - 1)
            if step in hooks:
                hooks[step]()
            if step >= LAG and step - LAG not in NEAR_AT:
                stage2(step - LAG)

        for n, j in enumerate(FAR_AT):
            landed(zrecv.at[n], s_ch2.at[j], r_ch2.at[j])
        total = res[...]
        for n in range(5):
            total = total + zrecv[n].astype(F32)
        res[...] = total

        def drain():
            for j in range(8):
                to_mate(j).wait_send()
                if j not in NEAR_AT:
                    for i in range(3):
                        to_y(j, i).wait_send()
                if j < 7:
                    to_z(j).wait_send()

        return drain

    def small(src, dst, ssem, rsem, i):
        return remote(src, dst, ssem.at[i], rsem.at[i], f, gs[YD[i]])

    def small_landed(dst, ssem, rsem):
        for i, d in enumerate(YD):
            ref = dst(gs[(4 - d) % 4])
            remote(ref, ref, ssem.at[i], rsem.at[i], f, gs[1]).wait_recv()

    def h_copy(i):
        return small(hx.at[g], hx.at[g], s_h, r_h, i)

    def c_copy(i):
        return small(cx.at[g], cx.at[g], s_c, r_c, i)

    def w_copy(i):
        return small(w2.at[c, g], w2.at[c, g], s_w, r_w, i)

    def w_mate(i):
        unit = w2.at[c, gs[(4 - YD[i]) % 4]]
        return remote(unit, unit, s_wp.at[i], r_wp.at[i], mate)

    def a_copy(i):
        return small(ax.at[g], ax.at[g], s_a, r_a, i)

    def n1_copy(d):
        return remote(ch.at[zs[d]], cr1.at[d - 1], s_n1.at[d - 1], r_n1.at[d - 1], zpeer[d])

    def n2_copy(d):
        return remote(cs, cr2.at[d - 1], s_n2.at[d - 1], r_n2.at[d - 1], qpeer[d])

    inputs = [
        pltpu.make_async_copy(src, dst, s_in.at[n])
        for n, (src, dst) in enumerate(
            (
                (table_ref, tab.at[c, z, y]),
                (x_ref, xs.at[g]),
                (h_ref, hx.at[g]),
                (cot_ref, cx.at[g]),
                (w_self_ref, w2.at[0, g]),
                (w_neigh_ref, w2.at[1, g]),
                (w_msg_ref, wm),
            )
        )
    ]
    for copy in inputs:
        copy.start()
    keys_v[0] = key_tile(dim_own_ref, dim_slot_ref)
    keys_v[1] = key_tile(ent_own_ref, ent_slot_ref)
    to_keys = [
        pltpu.make_async_copy(keys_v.at[0], keys_dim, s_in.at[7]),
        pltpu.make_async_copy(keys_v.at[1], keys_ent, s_in.at[8]),
    ]
    for copy in to_keys:
        copy.start()
    prepare(dim_own_ref, dim_slot_ref, None, bt_dim, ot_dim)
    prepare(ent_own_ref, ent_slot_ref, b_ent, bt_ent, ot_ent)
    owner_no = lax.broadcasted_iota(jnp.int32, (64, W), 0).astype(F32)
    hits = jnp.zeros((64, W), F32)
    for i in range(ROWS // W):
        orow = jnp.broadcast_to(ent_own_ref[i : i + 1, :].astype(F32), (64, W))
        named = jnp.where(orow == owner_no, 1.0, 0.0).astype(BF)
        hits = hits + jnp.dot(named, b_ent[i * W : (i + 1) * W, :], preferred_element_type=F32)
    ch[...] = hits.reshape(8, 8, W)
    for copy in inputs + to_keys:
        copy.wait()
    pl.semaphore_wait(barrier, len(friends))
    gather_open()
    for n in range(2):
        x_copy(n).start()
    for n in range(2):
        x_copy(n).wait_send()
        x_copy(n + 2).start()
    gather_near()
    for d in range(1, 8):
        n1_copy(d).start()

    def relay_x():
        x_landed(0)
        x_copy(4).start()
        x_landed(1)
        x_copy(5).start()

    def keep(rows, found):
        acc[rows, :] = found

    gather_run(keys_dim, keep, {0: relay_x})

    for n in range(2, 6):
        x_landed(n)
    for i in range(3):
        h_copy(i).start()
        c_copy(i).start()
        w_copy(i).start()

    def message_tile(t, carry):
        rows = pl.ds(pl.multiple_of(t * TILE, TILE), TILE)
        feats = jnp.concatenate([xs[b, rows, :] for b in range(4)], axis=1)
        v = acc[rows, :] + jnp.dot(feats, wm[...], preferred_element_type=F32)
        s = sigmoid_of(v)
        val[rows, :] = (v * s).astype(BF)
        slope[rows, :] = s * (1.0 + v * (1.0 - s))
        return carry

    lax.fori_loop(0, ROWS // TILE, message_tile, 0)
    gather_drain()

    for d in range(1, 8):
        ref = cr1.at[d - 1]
        landed(ref, s_n1.at[d - 1], r_n1.at[d - 1])
    zsum = ch[z]
    for d in range(1, 8):
        zsum = zsum + cr1[d - 1]
    cs[...] = zsum
    for d in range(1, 8):
        n2_copy(d).start()

    def weights_on():
        small_landed(lambda b: w2.at[c, b], s_w, r_w)
        for i in range(3):
            w_mate(i).start()

    def from_entities():
        small_landed(lambda b: hx.at[b], s_h, r_h)
        small_landed(lambda b: cx.at[b], s_c, r_c)
        for i, d in enumerate(YD):
            ref = w2.at[1 - c, gs[(4 - d) % 4]]
            landed(ref, s_wp.at[i], r_wp.at[i])
        h_full = jnp.concatenate([hx[b] for b in range(4)], axis=1)
        for b in range(4):
            pre[b] = jnp.dot(h_full, w2[0, b], preferred_element_type=F32)

    drain1 = reduce_all(
        val,
        psend1,
        precv1,
        gsend1,
        grecv1,
        ysend1,
        yrecv1,
        zsend1,
        zrecv1,
        res1,
        False,
        {8: weights_on, 10: from_entities},
    )

    for d in range(1, 8):
        landed(cr2.at[d - 1], s_n2.at[d - 1], r_n2.at[d - 1])
    hsum = cs[...]
    for d in range(1, 8):
        hsum = hsum + cr2[d - 1]
    row_no = lax.broadcasted_iota(jnp.int32, (8, W), 0)
    mine_row = jnp.sum(jnp.where(row_no == q, hsum, 0.0), axis=0, keepdims=True)
    column = jnp.sum(
        jnp.where(eye, jnp.broadcast_to(mine_row, (W, W)), 0.0), axis=1, keepdims=True
    )
    div[...] = jnp.broadcast_to(jnp.maximum(column, 1.0), (W, W))

    ax[g] = (res1[...] / div[...]).astype(BF)
    for i in range(3):
        a_copy(i).start()
    drain1()
    small_landed(lambda b: ax.at[b], s_a, r_a)
    a_full = jnp.concatenate([ax[b] for b in range(4)], axis=1)
    d_agg = jnp.zeros((W, W), F32)
    mine_rows = pl.ds(pl.multiple_of(g * W, W), W)
    for b in range(4):
        v = pre[b] + jnp.dot(a_full, w2[1, b], preferred_element_type=F32)
        pre[b] = v
        s = sigmoid_of(v)
        d_pre = (cx[b].astype(F32) * (s * (1.0 + v * (1.0 - s)))).astype(BF)
        d_agg = d_agg + lax.dot_general(
            d_pre, w2[1, b, mine_rows, :], (((1,), (1,)), ((), ())), preferred_element_type=F32
        )
    tab[c, z, y] = (d_agg / div[...]).astype(BF)
    gather_open()
    v = pre[g]
    s = sigmoid_of(v)
    out_ref[...] = (v * s).astype(BF)
    d_pre = (cx[g].astype(F32) * (s * (1.0 + v * (1.0 - s)))).astype(BF)
    for b in range(4):
        span = slice(b * W, (b + 1) * W)
        gw[1, span, :] = lax.dot_general(
            hx[b], d_pre, (((0,), (0,)), ((), ())), preferred_element_type=F32
        )
        gw[2, span, :] = lax.dot_general(
            ax[b], d_pre, (((0,), (0,)), ((), ())), preferred_element_type=F32
        )

    gather_near()
    def back(rows, found):
        val[rows, :] = (found * slope[rows, :]).astype(BF)

    gather_run(keys_ent, back, {})
    gather_drain()
    for b in range(4):
        gw[0, b * W : (b + 1) * W, :] = lax.dot_general(
            xs[b], val[...], (((0,), (0,)), ((), ())), preferred_element_type=F32
        )
    drain2 = reduce_all(
        val,
        psend2,
        precv2,
        gsend2,
        grecv2,
        ysend2,
        yrecv2,
        zsend2,
        zrecv2,
        res2,
        True,
        {},
    )
    sums_ref[...] = res2[...]

    drain2()
    for n in range(2, 6):
        x_copy(n).wait_send()
    for i in range(3):
        h_copy(i).wait_send()
        c_copy(i).wait_send()
        w_copy(i).wait_send()
        w_mate(i).wait_send()
        a_copy(i).wait_send()
    for d in range(1, 8):
        n1_copy(d).wait_send()
        n2_copy(d).wait_send()


def hand_out(out_in, sums_in, out_ref, gwm_ref, gws_ref, gwn_ref, gdim_ref):
    out_ref[...] = out_in[...]
    gdim_ref[...] = sums_in[0:W]
    gwm_ref[...] = sums_in[W : W + 8]
    gws_ref[...] = sums_in[W + 8 : W + 16]
    gwn_ref[...] = sums_in[W + 16 : W + 24]


def shards(x, dim_owner, dim_slot, fact_owner, fact_slot, table, h, w_msg, w_self, w_neigh, cot):
    tile = (ROWS // W, W)
    vmem = pl.BlockSpec(memory_space=pltpu.VMEM)
    anywhere = pl.BlockSpec(memory_space=pl.ANY)
    dma = pltpu.SemaphoreType.DMA

    def lots(tall, *lead):
        return pltpu.VMEM((*lead, tall, W), BF)

    def stages(tall):
        return [
            lots(tall, 8, NY),
            lots(tall, 8, NY),
            lots(tall, 2, NY),
            lots(tall, 2, NY),
            lots(tall, 6, 3),
            lots(tall, 6, 3),
            lots(tall, 5),
            lots(tall, 5),
        ]

    def sems(*shape):
        return [dma(shape), dma(shape)]

    scratch = [
        lots(ROWS, 4),
        lots(W, 2, NZ, NY),
        pltpu.VMEM((ROWS, W), BF),
        pltpu.VMEM((W, ROWS), BF),
        pltpu.VMEM((W, ROWS), BF),
        pltpu.VMEM((W, ROWS), BF),
        pltpu.VMEM((W, ROWS), BF),
        pltpu.VMEM((ROWS, W), F32),
        pltpu.VMEM((ROWS, W), F32),
        pltpu.VMEM((ROWS, W), BF),
        pltpu.VMEM((8, 8, W), F32),
        pltpu.VMEM((8, W), F32),
        pltpu.VMEM((7, 8, W), F32),
        pltpu.VMEM((7, 8, W), F32),
        lots(W, 4),
        lots(W, 4),
        lots(W, 4),
        lots(512, 2, 4),
        lots(512),
        pltpu.VMEM((4, W, W), F32),
        pltpu.VMEM((3, 512, W), F32),
        pltpu.VMEM((8, NY, EXTRA, W), F32),
        pltpu.VMEM((8, EXTRA, W), F32),
        *stages(W),
        *stages(EXTRA),
        pltpu.VMEM((W, W), F32),
        pltpu.VMEM((EXTRA, W), F32),
        pltpu.VMEM((W, W), F32),
        *sems(9),
        *sems(8, 3),
        *sems(8),
        *sems(9),
        *sems(8, 3),
        *sems(8),
        *sems(6),
        *sems(3),
        *sems(3),
        *sems(3),
        *sems(3),
        *sems(3),
        *sems(7),
        *sems(7),
        dma((9,)),
        pltpu.VMEM((2, ROWS // W, W), jnp.int32),
        pltpu.SMEM((ROWS // W, W), jnp.int32),
        pltpu.SMEM((ROWS // W, W), jnp.int32),
        pltpu.VMEM((2 * NZ * NY * W, W), F32),
    ]
    out, sums = pl.pallas_call(
        kernel,
        out_shape=(
            jax.ShapeDtypeStruct((W, W), BF),
            jax.ShapeDtypeStruct((EXTRA, W), F32),
        ),
        in_specs=[anywhere] + [vmem] * 4 + [anywhere] * 6,
        out_specs=(vmem,) * 2,
        scratch_shapes=scratch,
        compiler_params=pltpu.CompilerParams(
            collective_id=0, has_side_effects=True, vmem_limit_bytes=56 * 1024 * 1024
        ),
    )(
        x,
        dim_owner.reshape(tile),
        dim_slot.reshape(tile),
        fact_owner.reshape(tile),
        fact_slot.reshape(tile),
        table,
        h,
        w_msg,
        w_self,
        w_neigh,
        cot,
    )
    return pl.pallas_call(
        hand_out,
        out_shape=(
            jax.ShapeDtypeStruct((W, W), BF),
            jax.ShapeDtypeStruct((8, W), F32),
            jax.ShapeDtypeStruct((8, W), F32),
            jax.ShapeDtypeStruct((8, W), F32),
            jax.ShapeDtypeStruct((W, W), F32),
        ),
        in_specs=[vmem] * 2,
        out_specs=(vmem,) * 5,
    )(out, sums)


def solution(mesh):
    placed = (
        P("fact", "feat"),
        P("fact", None),
        P("fact"),
        P("fact", None),
        P("fact"),
        P("fact", "feat"),
        P("fact", "feat"),
        P(None, "feat"),
        P(None, "feat"),
        P(None, "feat"),
        P("fact", "feat"),
    )
    return jax.shard_map(
        shards,
        mesh=mesh,
        in_specs=placed,
        out_specs=(P("fact", "feat"),) * 5,
        check_vma=False,
    )
```

```python
import jax
import jax.numpy as jnp
from jax import lax
from jax.experimental import pallas as pl
from jax.experimental.pallas import tpu as pltpu
from jax.sharding import PartitionSpec as P

MESH = pl.DeviceIdType.MESH
BF = jnp.bfloat16
F32 = jnp.float32

NZ, NY = 8, 4
EVENTS = (0, -2, 2, -3, 3, 4, -1, 1)
FAR = 6
TARGETS = (4, -3, 1, -1, 3, -2, 2, 0)
NEAR_AT = (2, 3)
FAR_AT = (0, 1, 4, 5, 6)
YD = (2, 1, 3)
ROWS = 1024
TILE = 256
W = 128
EXTRA = 160
LAG = 5


def sigmoid_of(v):
    return 1.0 / (1.0 + jnp.exp(-v))


def kernel(
    x_ref,
    dim_own_ref,
    dim_slot_ref,
    ent_own_ref,
    ent_slot_ref,
    table_ref,
    h_ref,
    w_msg_ref,
    w_self_ref,
    w_neigh_ref,
    cot_ref,
    out_ref,
    sums_ref,
    xs,
    tab,
    b_ent,
    bt_dim,
    bt_ent,
    ot_dim,
    ot_ent,
    acc,
    slope,
    val,
    ch,
    cs,
    cr1,
    cr2,
    hx,
    cx,
    ax,
    w2,
    wm,
    pre,
    gw,
    pown,
    yown,
    psend1,
    precv1,
    gsend1,
    grecv1,
    ysend1,
    yrecv1,
    zsend1,
    zrecv1,
    psend2,
    precv2,
    gsend2,
    grecv2,
    ysend2,
    yrecv2,
    zsend2,
    zrecv2,
    res1,
    res2,
    div,
    s_ch,
    r_ch,
    s_y,
    r_y,
    s_p,
    r_p,
    s_ch2,
    r_ch2,
    s_y2,
    r_y2,
    s_p2,
    r_p2,
    s_x,
    r_x,
    s_h,
    r_h,
    s_c,
    r_c,
    s_w,
    r_w,
    s_wp,
    r_wp,
    s_a,
    r_a,
    s_n1,
    r_n1,
    s_n2,
    r_n2,
    s_in,
    keys_v,
    keys_dim,
    keys_ent,
    wide,
):
    f = lax.axis_index("fact")
    g = lax.axis_index("feat")
    z, y, c = f // 8, lax.rem(f // 2, 4), lax.rem(f, 2)
    q = lax.rem(f, 8)

    def at(zz, yy, cc):
        return (zz * 4 + yy) * 2 + cc

    zs = [lax.rem(z + d, NZ) for d in range(NZ)]
    ys = [lax.rem(y + d, NY) for d in range(NY)]
    gs = [lax.rem(g + d, 4) for d in range(4)]
    right, left, mate = at(zs[1], y, c), at(zs[7], y, c), at(z, y, 1 - c)
    zpeer = [at(zs[d], y, c) for d in range(NZ)]
    ypeer = [at(z, ys[d], c) for d in YD]
    qpeer = [z * 8 + lax.rem(q + d, 8) for d in range(8)]

    def remote(src, dst, ssem, rsem, to_f, to_g=None):
        return pltpu.make_async_remote_copy(
            src_ref=src,
            dst_ref=dst,
            send_sem=ssem,
            recv_sem=rsem,
            device_id=(to_f, g if to_g is None else to_g),
            device_id_type=MESH,
        )

    barrier = pltpu.get_barrier_semaphore()
    friends = [(p, g) for p in zpeer[1:]] + [(p, g) for p in qpeer[1:]] + [(f, p) for p in gs[1:]]
    for friend in friends:
        pl.semaphore_signal(barrier, inc=1, device_id=friend, device_id_type=MESH)

    half = [pl.ds(0, ROWS // 2), pl.ds(ROWS // 2, ROWS // 2)]

    def x_copy(n):
        if n < 4:
            to, part = ((1, 0), (3, 1), (1, 1), (3, 0))[n]
            src = xs.at[g, half[part]]
            dst = src
        elif n == 4:
            to, src = 1, xs.at[gs[3], half[0]]
            dst = src
        else:
            to, src = 3, xs.at[gs[1], half[1]]
            dst = src
        return remote(src, dst, s_x.at[n], r_x.at[n], f, gs[to])

    def x_landed(n):
        block, part = ((3, 0), (1, 1), (3, 1), (1, 0), (2, 0), (2, 1))[n]
        dst = xs.at[gs[block], half[part]]
        remote(dst, dst, s_x.at[n], r_x.at[n], f, gs[1]).wait_recv()

    def unit(k):
        return tab.at[c, zs[EVENTS[k] % NZ], y]

    def group(k):
        return tab.at[c, zs[EVENTS[k] % NZ]]

    def z_send(k):
        piece = unit(0) if k < FAR else group(0)
        return remote(piece, piece, s_ch.at[k], r_ch.at[k], zpeer[-EVENTS[k] % NZ])

    def y_send(k, i):
        return remote(unit(k), unit(k), s_y.at[k, i], r_y.at[k, i], ypeer[i])

    def p_send(k):
        return remote(group(k), group(k), s_p.at[k], r_p.at[k], mate)

    def landed(dst, ssem, rsem):
        remote(dst, dst, ssem, rsem, mate).wait_recv()

    def gather_open():
        for k in range(1, FAR):
            z_send(k).start()
        for i in range(3):
            y_send(0, i).start()

    def gather_near():
        gather_join(0)
        for k in (6, 7):
            z_send(k).start()

    def gather_spread(k):
        landed(unit(k), s_ch.at[k], r_ch.at[k])
        for i in range(3):
            y_send(k, i).start()

    def gather_join(k):
        zk = zs[EVENTS[k] % NZ]
        if k < FAR:
            for i, d in enumerate(YD):
                landed(tab.at[c, zk, ys[(NY - d) % NY]], s_y.at[k, i], r_y.at[k, i])
        else:
            landed(group(k), s_ch.at[k], r_ch.at[k])
        p_send(k).start()

    def gather_drain():
        for k in range(8):
            if k > 0:
                z_send(k).wait_send()
            if k < FAR:
                for i in range(3):
                    y_send(k, i).wait_send()
            p_send(k).wait_send()

    def gather_run(keys, sink, hooks):
        def use(k):
            zk = zs[EVENTS[k] % NZ]
            landed(tab.at[1 - c, zk], s_p.at[k], r_p.at[k])
            for parity in (0, 1):
                first = parity * NZ * NY * W + zk * (NY * W)
                rows = pl.ds(pl.multiple_of(first, NY * W), NY * W)
                wide[rows, :] = tab[parity, zk].reshape(NY * W, W).astype(F32)

        plan = (
            (gather_spread, 1),
            (gather_spread, 2),
            (use, 0),
            (gather_spread, 3),
            (gather_spread, 4),
            (gather_spread, 5),
            (gather_join, 1),
            (gather_join, 2),
            (gather_join, 6),
            (gather_join, 7),
            (gather_join, 3),
            (gather_join, 4),
            (use, 1),
            (use, 2),
            (use, 6),
            (use, 7),
            (gather_join, 5),
            (use, 3),
            (use, 4),
            (use, 5),
        )
        for n, (stage, k) in enumerate(plan):
            if n in hooks:
                hooks[n]()
            stage(k)

        def some(t, carry):
            i, first = t // 4, lax.rem(t, 4) * 32
            found = [wide[pl.ds(keys[i, first + j], 1), :] for j in range(32)]
            sink(pl.ds(pl.multiple_of(t * 32, 32), 32), jnp.concatenate(found, axis=0))
            return carry

        lax.fori_loop(0, ROWS // 32, some, 0)

    def key_tile(own_ref, slot_ref):
        owns = own_ref[...]
        return lax.rem(owns, 2) * (NZ * NY * W) + (owns // 2) * W + slot_ref[...]

    def lane_rows(index_ref, i):
        return jnp.broadcast_to(index_ref[i : i + 1, :].astype(F32), (W, W))

    sub = lax.broadcasted_iota(jnp.int32, (W, W), 0)
    lane = lax.broadcasted_iota(jnp.int32, (W, W), 1)
    eye = sub == lane
    subf, lanef = sub.astype(F32), lane.astype(F32)
    ones_w = jnp.ones((W, W), BF)

    def prepare(own_ref, slot_ref, slots, slots_t, owners_t):
        for i in range(ROWS // W):
            span = slice(i * W, (i + 1) * W)
            srow = lane_rows(slot_ref, i)
            slots_t[:, span] = jnp.where(srow == subf, 1.0, 0.0).astype(BF)
            if slots is not None:
                scol = jnp.dot(
                    jnp.where(eye, srow, 0.0).astype(BF), ones_w, preferred_element_type=F32
                )
                slots[span, :] = jnp.where(scol == lanef, 1.0, 0.0).astype(BF)
            oint = own_ref[i : i + 1, :]
            flipped = oint + c * (1 - 2 * lax.rem(oint, 2))
            owners_t[:, span] = jnp.broadcast_to(flipped.astype(F32), (W, W)).astype(BF)

    def reduce_block(j, source, psend, grads):
        tz = zs[TARGETS[j] % NZ]
        owners_t, slots_t = (ot_dim, bt_dim) if grads else (ot_ent, bt_ent)

        base = (tz * 8).astype(F32)
        rel = owners_t[...] - jnp.full((W, ROWS), base, F32).astype(BF)
        ones = slots_t[...]
        zero = jnp.zeros_like(ones)
        lhs = jnp.concatenate(
            [
                jnp.where(rel == jnp.asarray(yy * 2 + side, BF), ones, zero)
                for side in (1, 0)
                for yy in range(NY)
            ],
            axis=0,
        )
        got = jnp.dot(lhs, source[...], preferred_element_type=F32)
        for yy in range(NY):
            psend[j, yy, 0:W] = got[yy * W : (yy + 1) * W].astype(BF)
            pown[j, yy, 0:W] = got[(NY + yy) * W : (NY + yy + 1) * W]
        if grads:
            blank = jnp.zeros((8, W), F32)
            for yy in range(NY):
                first = tz * 8 + yy * 2
                mine = pl.ds(pl.multiple_of((first + c) * 8, 8), 8)
                other = pl.ds(pl.multiple_of((first + 1 - c) * 8, 8), 8)
                for n in range(3):
                    pown[j, yy, W + 8 * n : W + 8 * n + 8] = gw[n, mine, :]
                pown[j, yy, W + 24 : W + 32] = blank
                psend[j, yy, W : W + 16] = jnp.concatenate(
                    [gw[0, other, :], gw[1, other, :]], axis=0
                ).astype(BF)
                psend[j, yy, W + 16 : W + 32] = jnp.concatenate(
                    [gw[2, other, :], blank], axis=0
                ).astype(BF)

    def reduce_all(
        source, psend, precv, gsend, grecv, ysend, yrecv, zsend, zrecv, res, grads, hooks
    ):
        tall = pl.ds(0, EXTRA if grads else W)

        def to_mate(j):
            return remote(psend.at[j], precv.at[j], s_p2.at[j], r_p2.at[j], mate)

        def slot(j):
            return 5 if j == 7 else FAR_AT.index(j)

        def to_y(j, i):
            n = slot(j)
            return remote(ysend.at[n, i], yrecv.at[n, i], s_y2.at[n, i], r_y2.at[n, i], ypeer[i])

        def to_z(j):
            to = zpeer[TARGETS[j] % NZ]
            if j in NEAR_AT:
                n = NEAR_AT.index(j)
                return remote(gsend.at[n], grecv.at[n], s_ch2.at[j], r_ch2.at[j], to)
            n = slot(j)
            return remote(zsend.at[n], zrecv.at[n], s_ch2.at[j], r_ch2.at[j], to)

        def stage1(j):
            landed(precv.at[j], s_p2.at[j], r_p2.at[j])
            if j in NEAR_AT:
                gsend[NEAR_AT.index(j)] = (pown[j, :, tall] + precv[j].astype(F32)).astype(BF)
                to_z(j).start()
                return
            if j == 7:
                for n in range(2):
                    landed(grecv.at[n], s_ch2.at[NEAR_AT[n]], r_ch2.at[NEAR_AT[n]])

            def block(yy):
                got = pown[j, yy, tall] + precv[j, yy].astype(F32)
                if j == 7:
                    for n in range(2):
                        got = got + grecv[n, yy].astype(F32)
                return got

            for i, d in enumerate(YD):
                ysend[slot(j), i] = block(ys[d]).astype(BF)
                to_y(j, i).start()
            yown[j, tall] = block(y)

        def stage2(j):
            for i in range(3):
                n = slot(j)
                landed(yrecv.at[n, i], s_y2.at[n, i], r_y2.at[n, i])
            total = yown[j, tall]
            for i in range(3):
                total = total + yrecv[slot(j), i].astype(F32)
            if j < 7:
                zsend[slot(j)] = total.astype(BF)
                to_z(j).start()
            else:
                res[...] = total

        for step in range(8 + LAG):
            if step < 8:
                reduce_block(step, source, psend, grads)
                to_mate(step).start()
            if 1 <= step < 9:
                stage1(step - 1)
            if step in hooks:
                hooks[step]()
            if step >= LAG and step - LAG not in NEAR_AT:
                stage2(step - LAG)

        for n, j in enumerate(FAR_AT):
            landed(zrecv.at[n], s_ch2.at[j], r_ch2.at[j])
        total = res[...]
        for n in range(5):
            total = total + zrecv[n].astype(F32)
        res[...] = total

        def drain():
            for j in range(8):
                to_mate(j).wait_send()
                if j not in NEAR_AT:
                    for i in range(3):
                        to_y(j, i).wait_send()
                if j < 7:
                    to_z(j).wait_send()

        return drain

    def small(src, dst, ssem, rsem, i):
        return remote(src, dst, ssem.at[i], rsem.at[i], f, gs[YD[i]])

    def small_landed(dst, ssem, rsem):
        for i, d in enumerate(YD):
            ref = dst(gs[(4 - d) % 4])
            remote(ref, ref, ssem.at[i], rsem.at[i], f, gs[1]).wait_recv()

    def h_copy(i):
        return small(hx.at[g], hx.at[g], s_h, r_h, i)

    def c_copy(i):
        return small(cx.at[g], cx.at[g], s_c, r_c, i)

    def w_copy(i):
        return small(w2.at[c, g], w2.at[c, g], s_w, r_w, i)

    def w_mate(i):
        unit = w2.at[c, gs[(4 - YD[i]) % 4]]
        return remote(unit, unit, s_wp.at[i], r_wp.at[i], mate)

    def a_copy(i):
        return small(ax.at[g], ax.at[g], s_a, r_a, i)

    def n1_copy(d):
        return remote(ch.at[zs[d]], cr1.at[d - 1], s_n1.at[d - 1], r_n1.at[d - 1], zpeer[d])

    def n2_copy(d):
        return remote(cs, cr2.at[d - 1], s_n2.at[d - 1], r_n2.at[d - 1], qpeer[d])

    inputs = [
        pltpu.make_async_copy(src, dst, s_in.at[n])
        for n, (src, dst) in enumerate(
            (
                (table_ref, tab.at[c, z, y]),
                (x_ref, xs.at[g]),
                (h_ref, hx.at[g]),
                (cot_ref, cx.at[g]),
                (w_self_ref, w2.at[0, g]),
                (w_neigh_ref, w2.at[1, g]),
                (w_msg_ref, wm),
            )
        )
    ]
    for copy in inputs:
        copy.start()
    keys_v[0] = key_tile(dim_own_ref, dim_slot_ref)
    keys_v[1] = key_tile(ent_own_ref, ent_slot_ref)
    to_keys = [
        pltpu.make_async_copy(keys_v.at[0], keys_dim, s_in.at[7]),
        pltpu.make_async_copy(keys_v.at[1], keys_ent, s_in.at[8]),
    ]
    for copy in to_keys:
        copy.start()
    prepare(dim_own_ref, dim_slot_ref, None, bt_dim, ot_dim)
    prepare(ent_own_ref, ent_slot_ref, b_ent, bt_ent, ot_ent)
    owner_no = lax.broadcasted_iota(jnp.int32, (64, W), 0).astype(F32)
    hits = jnp.zeros((64, W), F32)
    for i in range(ROWS // W):
        orow = jnp.broadcast_to(ent_own_ref[i : i + 1, :].astype(F32), (64, W))
        named = jnp.where(orow == owner_no, 1.0, 0.0).astype(BF)
        hits = hits + jnp.dot(named, b_ent[i * W : (i + 1) * W, :], preferred_element_type=F32)
    ch[...] = hits.reshape(8, 8, W)
    for copy in inputs + to_keys:
        copy.wait()
    pl.semaphore_wait(barrier, len(friends))
    gather_open()
    for n in range(2):
        x_copy(n).start()
    for n in range(2):
        x_copy(n).wait_send()
        x_copy(n + 2).start()
    gather_near()
    for d in range(1, 8):
        n1_copy(d).start()

    def relay_x():
        x_landed(0)
        x_copy(4).start()
        x_landed(1)
        x_copy(5).start()

    def encode():
        for n in range(2, 6):
            x_landed(n)
        for i in range(3):
            h_copy(i).start()
            c_copy(i).start()
            w_copy(i).start()
        feats = jnp.concatenate([xs[b] for b in range(4)], axis=1)
        acc[...] = jnp.dot(feats, wm[...], preferred_element_type=F32)

    def message(rows, found):
        v = acc[rows, :] + found
        s = sigmoid_of(v)
        val[rows, :] = (v * s).astype(BF)
        slope[rows, :] = s * (1.0 + v * (1.0 - s))

    gather_run(keys_dim, message, {0: relay_x, 17: encode})
    gather_drain()

    for d in range(1, 8):
        ref = cr1.at[d - 1]
        landed(ref, s_n1.at[d - 1], r_n1.at[d - 1])
    zsum = ch[z]
    for d in range(1, 8):
        zsum = zsum + cr1[d - 1]
    cs[...] = zsum
    for d in range(1, 8):
        n2_copy(d).start()

    def weights_on():
        small_landed(lambda b: w2.at[c, b], s_w, r_w)
        for i in range(3):
            w_mate(i).start()

    def from_entities():
        small_landed(lambda b: hx.at[b], s_h, r_h)
        small_landed(lambda b: cx.at[b], s_c, r_c)
        for i, d in enumerate(YD):
            ref = w2.at[1 - c, gs[(4 - d) % 4]]
            landed(ref, s_wp.at[i], r_wp.at[i])
        h_full = jnp.concatenate([hx[b] for b in range(4)], axis=1)
        for b in range(4):
            pre[b] = jnp.dot(h_full, w2[0, b], preferred_element_type=F32)

    def divide_by():
        for d in range(1, 8):
            landed(cr2.at[d - 1], s_n2.at[d - 1], r_n2.at[d - 1])
        hsum = cs[...]
        for d in range(1, 8):
            hsum = hsum + cr2[d - 1]
        row_no = lax.broadcasted_iota(jnp.int32, (8, W), 0)
        mine_row = jnp.sum(jnp.where(row_no == q, hsum, 0.0), axis=0, keepdims=True)
        column = jnp.sum(
            jnp.where(eye, jnp.broadcast_to(mine_row, (W, W)), 0.0), axis=1, keepdims=True
        )
        div[...] = jnp.broadcast_to(jnp.maximum(column, 1.0), (W, W))

    drain1 = reduce_all(
        val,
        psend1,
        precv1,
        gsend1,
        grecv1,
        ysend1,
        yrecv1,
        zsend1,
        zrecv1,
        res1,
        False,
        {8: weights_on, 9: divide_by, 10: from_entities},
    )

    ax[g] = (res1[...] / div[...]).astype(BF)
    for i in range(3):
        a_copy(i).start()
    drain1()
    small_landed(lambda b: ax.at[b], s_a, r_a)
    a_full = jnp.concatenate([ax[b] for b in range(4)], axis=1)
    d_agg = jnp.zeros((W, W), F32)
    mine_rows = pl.ds(pl.multiple_of(g * W, W), W)
    for b in range(4):
        v = pre[b] + jnp.dot(a_full, w2[1, b], preferred_element_type=F32)
        pre[b] = v
        s = sigmoid_of(v)
        d_pre = (cx[b].astype(F32) * (s * (1.0 + v * (1.0 - s)))).astype(BF)
        d_agg = d_agg + lax.dot_general(
            d_pre, w2[1, b, mine_rows, :], (((1,), (1,)), ((), ())), preferred_element_type=F32
        )
    tab[c, z, y] = (d_agg / div[...]).astype(BF)
    gather_open()
    v = pre[g]
    s = sigmoid_of(v)
    out_ref[...] = (v * s).astype(BF)
    d_pre = (cx[g].astype(F32) * (s * (1.0 + v * (1.0 - s)))).astype(BF)
    for b in range(4):
        span = slice(b * W, (b + 1) * W)
        gw[1, span, :] = lax.dot_general(
            hx[b], d_pre, (((0,), (0,)), ((), ())), preferred_element_type=F32
        )
        gw[2, span, :] = lax.dot_general(
            ax[b], d_pre, (((0,), (0,)), ((), ())), preferred_element_type=F32
        )

    gather_near()
    def back(rows, found):
        val[rows, :] = (found * slope[rows, :]).astype(BF)

    gather_run(keys_ent, back, {})
    gather_drain()
    for b in range(4):
        gw[0, b * W : (b + 1) * W, :] = lax.dot_general(
            xs[b], val[...], (((0,), (0,)), ((), ())), preferred_element_type=F32
        )
    drain2 = reduce_all(
        val,
        psend2,
        precv2,
        gsend2,
        grecv2,
        ysend2,
        yrecv2,
        zsend2,
        zrecv2,
        res2,
        True,
        {},
    )
    sums_ref[...] = res2[...]

    drain2()
    for n in range(2, 6):
        x_copy(n).wait_send()
    for i in range(3):
        h_copy(i).wait_send()
        c_copy(i).wait_send()
        w_copy(i).wait_send()
        w_mate(i).wait_send()
        a_copy(i).wait_send()
    for d in range(1, 8):
        n1_copy(d).wait_send()
        n2_copy(d).wait_send()


def hand_out(out_in, sums_in, out_ref, gwm_ref, gws_ref, gwn_ref, gdim_ref):
    out_ref[...] = out_in[...]
    gdim_ref[...] = sums_in[0:W]
    gwm_ref[...] = sums_in[W : W + 8]
    gws_ref[...] = sums_in[W + 8 : W + 16]
    gwn_ref[...] = sums_in[W + 16 : W + 24]


def shards(x, dim_owner, dim_slot, fact_owner, fact_slot, table, h, w_msg, w_self, w_neigh, cot):
    tile = (ROWS // W, W)
    vmem = pl.BlockSpec(memory_space=pltpu.VMEM)
    anywhere = pl.BlockSpec(memory_space=pl.ANY)
    dma = pltpu.SemaphoreType.DMA

    def lots(tall, *lead):
        return pltpu.VMEM((*lead, tall, W), BF)

    def stages(tall):
        return [
            lots(tall, 8, NY),
            lots(tall, 8, NY),
            lots(tall, 2, NY),
            lots(tall, 2, NY),
            lots(tall, 6, 3),
            lots(tall, 6, 3),
            lots(tall, 5),
            lots(tall, 5),
        ]

    def sems(*shape):
        return [dma(shape), dma(shape)]

    scratch = [
        lots(ROWS, 4),
        lots(W, 2, NZ, NY),
        pltpu.VMEM((ROWS, W), BF),
        pltpu.VMEM((W, ROWS), BF),
        pltpu.VMEM((W, ROWS), BF),
        pltpu.VMEM((W, ROWS), BF),
        pltpu.VMEM((W, ROWS), BF),
        pltpu.VMEM((ROWS, W), F32),
        pltpu.VMEM((ROWS, W), F32),
        pltpu.VMEM((ROWS, W), BF),
        pltpu.VMEM((8, 8, W), F32),
        pltpu.VMEM((8, W), F32),
        pltpu.VMEM((7, 8, W), F32),
        pltpu.VMEM((7, 8, W), F32),
        lots(W, 4),
        lots(W, 4),
        lots(W, 4),
        lots(512, 2, 4),
        lots(512),
        pltpu.VMEM((4, W, W), F32),
        pltpu.VMEM((3, 512, W), F32),
        pltpu.VMEM((8, NY, EXTRA, W), F32),
        pltpu.VMEM((8, EXTRA, W), F32),
        *stages(W),
        *stages(EXTRA),
        pltpu.VMEM((W, W), F32),
        pltpu.VMEM((EXTRA, W), F32),
        pltpu.VMEM((W, W), F32),
        *sems(9),
        *sems(8, 3),
        *sems(8),
        *sems(9),
        *sems(8, 3),
        *sems(8),
        *sems(6),
        *sems(3),
        *sems(3),
        *sems(3),
        *sems(3),
        *sems(3),
        *sems(7),
        *sems(7),
        dma((9,)),
        pltpu.VMEM((2, ROWS // W, W), jnp.int32),
        pltpu.SMEM((ROWS // W, W), jnp.int32),
        pltpu.SMEM((ROWS // W, W), jnp.int32),
        pltpu.VMEM((2 * NZ * NY * W, W), F32),
    ]
    out, sums = pl.pallas_call(
        kernel,
        out_shape=(
            jax.ShapeDtypeStruct((W, W), BF),
            jax.ShapeDtypeStruct((EXTRA, W), F32),
        ),
        in_specs=[anywhere] + [vmem] * 4 + [anywhere] * 6,
        out_specs=(vmem,) * 2,
        scratch_shapes=scratch,
        compiler_params=pltpu.CompilerParams(
            collective_id=0, has_side_effects=True, vmem_limit_bytes=56 * 1024 * 1024
        ),
    )(
        x,
        dim_owner.reshape(tile),
        dim_slot.reshape(tile),
        fact_owner.reshape(tile),
        fact_slot.reshape(tile),
        table,
        h,
        w_msg,
        w_self,
        w_neigh,
        cot,
    )
    return pl.pallas_call(
        hand_out,
        out_shape=(
            jax.ShapeDtypeStruct((W, W), BF),
            jax.ShapeDtypeStruct((8, W), F32),
            jax.ShapeDtypeStruct((8, W), F32),
            jax.ShapeDtypeStruct((8, W), F32),
            jax.ShapeDtypeStruct((W, W), F32),
        ),
        in_specs=[vmem] * 2,
        out_specs=(vmem,) * 5,
    )(out, sums)


def solution(mesh):
    placed = (
        P("fact", "feat"),
        P("fact", None),
        P("fact"),
        P("fact", None),
        P("fact"),
        P("fact", "feat"),
        P("fact", "feat"),
        P(None, "feat"),
        P(None, "feat"),
        P(None, "feat"),
        P("fact", "feat"),
    )
    return jax.shard_map(
        shards,
        mesh=mesh,
        in_specs=placed,
        out_specs=(P("fact", "feat"),) * 5,
        check_vma=False,
    )
```

```python
import jax
import jax.numpy as jnp
from jax import lax
from jax.experimental import pallas as pl
from jax.experimental.pallas import tpu as pltpu
from jax.sharding import PartitionSpec as P

MESH = pl.DeviceIdType.MESH
BF = jnp.bfloat16
F32 = jnp.float32

NZ, NY = 8, 4
EVENTS = (0, -2, 2, -3, 3, 4, -1, 1)
FAR = 6
TARGETS = (4, -3, 1, -1, 3, -2, 2, 0)
NEAR_AT = (2, 3)
FAR_AT = (0, 1, 4, 5, 6)
YD = (2, 1, 3)
ROWS = 1024
TILE = 256
W = 128
EXTRA = 160
LAG = 5
SPLIT = (0, 6, 7)


def sigmoid_of(v):
    return 1.0 / (1.0 + jnp.exp(-v))


def kernel(
    x_ref,
    dim_own_ref,
    dim_slot_ref,
    ent_own_ref,
    ent_slot_ref,
    table_ref,
    h_ref,
    w_msg_ref,
    w_self_ref,
    w_neigh_ref,
    cot_ref,
    out_ref,
    sums_ref,
    xs,
    tab,
    b_ent,
    bt_dim,
    bt_ent,
    ot_dim,
    ot_ent,
    acc,
    slope,
    val,
    ch,
    cs,
    cr1,
    cr2,
    hx,
    cx,
    ax,
    w2,
    wm,
    pre,
    gw,
    pown,
    yown,
    psend1,
    precv1,
    gsend1,
    grecv1,
    ysend1,
    yrecv1,
    zsend1,
    zrecv1,
    psend2,
    precv2,
    gsend2,
    grecv2,
    ysend2,
    yrecv2,
    zsend2,
    zrecv2,
    res1,
    res2,
    div,
    s_ch,
    r_ch,
    s_y,
    r_y,
    s_p,
    r_p,
    s_ch2,
    r_ch2,
    s_y2,
    r_y2,
    s_p2,
    r_p2,
    s_x,
    r_x,
    s_h,
    r_h,
    s_c,
    r_c,
    s_w,
    r_w,
    s_wp,
    r_wp,
    s_a,
    r_a,
    s_n1,
    r_n1,
    s_n2,
    r_n2,
    s_in,
    keys_v,
    keys_dim,
    keys_ent,
    wide,
):
    f = lax.axis_index("fact")
    g = lax.axis_index("feat")
    z, y, c = f // 8, lax.rem(f // 2, 4), lax.rem(f, 2)
    q = lax.rem(f, 8)

    def at(zz, yy, cc):
        return (zz * 4 + yy) * 2 + cc

    zs = [lax.rem(z + d, NZ) for d in range(NZ)]
    ys = [lax.rem(y + d, NY) for d in range(NY)]
    gs = [lax.rem(g + d, 4) for d in range(4)]
    right, left, mate = at(zs[1], y, c), at(zs[7], y, c), at(z, y, 1 - c)
    zpeer = [at(zs[d], y, c) for d in range(NZ)]
    ypeer = [at(z, ys[d], c) for d in YD]
    qpeer = [z * 8 + lax.rem(q + d, 8) for d in range(8)]

    def remote(src, dst, ssem, rsem, to_f, to_g=None):
        return pltpu.make_async_remote_copy(
            src_ref=src,
            dst_ref=dst,
            send_sem=ssem,
            recv_sem=rsem,
            device_id=(to_f, g if to_g is None else to_g),
            device_id_type=MESH,
        )

    barrier = pltpu.get_barrier_semaphore()
    friends = [(p, g) for p in zpeer[1:]] + [(p, g) for p in qpeer[1:]] + [(f, p) for p in gs[1:]]
    for friend in friends:
        pl.semaphore_signal(barrier, inc=1, device_id=friend, device_id_type=MESH)

    half = [pl.ds(0, ROWS // 2), pl.ds(ROWS // 2, ROWS // 2)]

    def x_copy(n):
        if n < 4:
            to, part = ((1, 0), (3, 1), (1, 1), (3, 0))[n]
            src = xs.at[g, half[part]]
            dst = src
        elif n == 4:
            to, src = 1, xs.at[gs[3], half[0]]
            dst = src
        else:
            to, src = 3, xs.at[gs[1], half[1]]
            dst = src
        return remote(src, dst, s_x.at[n], r_x.at[n], f, gs[to])

    def x_landed(n):
        block, part = ((3, 0), (1, 1), (3, 1), (1, 0), (2, 0), (2, 1))[n]
        dst = xs.at[gs[block], half[part]]
        remote(dst, dst, s_x.at[n], r_x.at[n], f, gs[1]).wait_recv()

    def unit(k):
        return tab.at[c, zs[EVENTS[k] % NZ], y]

    def group(k):
        return tab.at[c, zs[EVENTS[k] % NZ]]

    def z_send(k):
        piece = unit(0) if k < FAR else group(0)
        return remote(piece, piece, s_ch.at[k], r_ch.at[k], zpeer[-EVENTS[k] % NZ])

    def y_send(k, i):
        return remote(unit(k), unit(k), s_y.at[k, i], r_y.at[k, i], ypeer[i])

    def p_send(k):
        return remote(group(k), group(k), s_p.at[k], r_p.at[k], mate)

    def landed(dst, ssem, rsem):
        remote(dst, dst, ssem, rsem, mate).wait_recv()

    def gather_open():
        for k in range(1, FAR):
            z_send(k).start()
        for i in range(3):
            y_send(0, i).start()

    def gather_near():
        gather_join(0)
        for k in (6, 7):
            z_send(k).start()

    def gather_spread(k):
        landed(unit(k), s_ch.at[k], r_ch.at[k])
        for i in range(3):
            y_send(k, i).start()

    def gather_join(k):
        zk = zs[EVENTS[k] % NZ]
        if k < FAR:
            for i, d in enumerate(YD):
                landed(tab.at[c, zk, ys[(NY - d) % NY]], s_y.at[k, i], r_y.at[k, i])
        else:
            landed(group(k), s_ch.at[k], r_ch.at[k])
        p_send(k).start()

    def gather_drain():
        for k in range(8):
            if k > 0:
                z_send(k).wait_send()
            if k < FAR:
                for i in range(3):
                    y_send(k, i).wait_send()
            p_send(k).wait_send()

    def gather_run(keys, sink, hooks):
        def use(k):
            zk = zs[EVENTS[k] % NZ]
            landed(tab.at[1 - c, zk], s_p.at[k], r_p.at[k])
            for parity in (0, 1):
                first = parity * NZ * NY * W + zk * (NY * W)
                rows = pl.ds(pl.multiple_of(first, NY * W), NY * W)
                wide[rows, :] = tab[parity, zk].reshape(NY * W, W).astype(F32)

        plan = (
            (gather_spread, 1),
            (gather_spread, 2),
            (use, 0),
            (gather_spread, 3),
            (gather_spread, 4),
            (gather_spread, 5),
            (gather_join, 1),
            (gather_join, 2),
            (gather_join, 6),
            (gather_join, 7),
            (gather_join, 3),
            (gather_join, 4),
            (use, 1),
            (use, 2),
            (use, 6),
            (use, 7),
            (gather_join, 5),
            (use, 3),
            (use, 4),
            (use, 5),
        )
        for n, (stage, k) in enumerate(plan):
            if n in hooks:
                hooks[n]()
            stage(k)

        def some(t, carry):
            i, first = t // 4, lax.rem(t, 4) * 32
            found = [wide[pl.ds(keys[i, first + j], 1), :] for j in range(32)]
            sink(pl.ds(pl.multiple_of(t * 32, 32), 32), jnp.concatenate(found, axis=0))
            return carry

        lax.fori_loop(0, ROWS // 32, some, 0)

    def key_tile(own_ref, slot_ref):
        owns = own_ref[...]
        return lax.rem(owns, 2) * (NZ * NY * W) + (owns // 2) * W + slot_ref[...]

    def lane_rows(index_ref, i):
        return jnp.broadcast_to(index_ref[i : i + 1, :].astype(F32), (W, W))

    sub = lax.broadcasted_iota(jnp.int32, (W, W), 0)
    lane = lax.broadcasted_iota(jnp.int32, (W, W), 1)
    eye = sub == lane
    subf, lanef = sub.astype(F32), lane.astype(F32)
    ones_w = jnp.ones((W, W), BF)

    def prepare(own_ref, slot_ref, slots, slots_t, owners_t):
        for i in range(ROWS // W):
            span = slice(i * W, (i + 1) * W)
            srow = lane_rows(slot_ref, i)
            slots_t[:, span] = jnp.where(srow == subf, 1.0, 0.0).astype(BF)
            if slots is not None:
                scol = jnp.dot(
                    jnp.where(eye, srow, 0.0).astype(BF), ones_w, preferred_element_type=F32
                )
                slots[span, :] = jnp.where(scol == lanef, 1.0, 0.0).astype(BF)
            oint = own_ref[i : i + 1, :]
            flipped = oint + c * (1 - 2 * lax.rem(oint, 2))
            owners_t[:, span] = jnp.broadcast_to(flipped.astype(F32), (W, W)).astype(BF)

    def reduce_block(j, source, psend, grads, send):
        tz = zs[TARGETS[j] % NZ]
        owners_t, slots_t = (ot_dim, bt_dim) if grads else (ot_ent, bt_ent)

        base = (tz * 8).astype(F32)
        rel = owners_t[...] - jnp.full((W, ROWS), base, F32).astype(BF)
        ones = slots_t[...]
        zero = jnp.zeros_like(ones)
        def product(sides):
            lhs = jnp.concatenate(
                [
                    jnp.where(rel == jnp.asarray(yy * 2 + side, BF), ones, zero)
                    for side in sides
                    for yy in range(NY)
                ],
                axis=0,
            )
            return jnp.dot(lhs, source[...], preferred_element_type=F32)

        def blocks(got, first):
            return [got[(first + yy) * W : (first + yy + 1) * W] for yy in range(NY)]

        if j in SPLIT:
            theirs = blocks(product((1,)), 0)
        else:
            got = product((1, 0))
            theirs, ours = blocks(got, 0), blocks(got, NY)
        for yy in range(NY):
            psend[j, yy, 0:W] = theirs[yy].astype(BF)
        if grads:
            blank = jnp.zeros((8, W), F32)
            for yy in range(NY):
                first = tz * 8 + yy * 2
                mine = pl.ds(pl.multiple_of((first + c) * 8, 8), 8)
                other = pl.ds(pl.multiple_of((first + 1 - c) * 8, 8), 8)
                for n in range(3):
                    pown[j, yy, W + 8 * n : W + 8 * n + 8] = gw[n, mine, :]
                pown[j, yy, W + 24 : W + 32] = blank
                psend[j, yy, W : W + 16] = jnp.concatenate(
                    [gw[0, other, :], gw[1, other, :]], axis=0
                ).astype(BF)
                psend[j, yy, W + 16 : W + 32] = jnp.concatenate(
                    [gw[2, other, :], blank], axis=0
                ).astype(BF)
        send()
        if j in SPLIT:
            ours = blocks(product((0,)), 0)
        for yy in range(NY):
            pown[j, yy, 0:W] = ours[yy]

    def reduce_all(
        source, psend, precv, gsend, grecv, ysend, yrecv, zsend, zrecv, res, grads, hooks
    ):
        tall = pl.ds(0, EXTRA if grads else W)

        def to_mate(j):
            return remote(psend.at[j], precv.at[j], s_p2.at[j], r_p2.at[j], mate)

        def slot(j):
            return 5 if j == 7 else FAR_AT.index(j)

        def to_y(j, i):
            n = slot(j)
            return remote(ysend.at[n, i], yrecv.at[n, i], s_y2.at[n, i], r_y2.at[n, i], ypeer[i])

        def to_z(j):
            to = zpeer[TARGETS[j] % NZ]
            if j in NEAR_AT:
                n = NEAR_AT.index(j)
                return remote(gsend.at[n], grecv.at[n], s_ch2.at[j], r_ch2.at[j], to)
            n = slot(j)
            return remote(zsend.at[n], zrecv.at[n], s_ch2.at[j], r_ch2.at[j], to)

        def stage1(j):
            landed(precv.at[j], s_p2.at[j], r_p2.at[j])
            if j in NEAR_AT:
                gsend[NEAR_AT.index(j)] = (pown[j, :, tall] + precv[j].astype(F32)).astype(BF)
                to_z(j).start()
                return
            if j == 7:
                for n in range(2):
                    landed(grecv.at[n], s_ch2.at[NEAR_AT[n]], r_ch2.at[NEAR_AT[n]])

            def block(yy):
                got = pown[j, yy, tall] + precv[j, yy].astype(F32)
                if j == 7:
                    for n in range(2):
                        got = got + grecv[n, yy].astype(F32)
                return got

            for i, d in enumerate(YD):
                ysend[slot(j), i] = block(ys[d]).astype(BF)
                to_y(j, i).start()
            yown[j, tall] = block(y)

        def stage2(j):
            for i in range(3):
                n = slot(j)
                landed(yrecv.at[n, i], s_y2.at[n, i], r_y2.at[n, i])
            total = yown[j, tall]
            for i in range(3):
                total = total + yrecv[slot(j), i].astype(F32)
            if j < 7:
                zsend[slot(j)] = total.astype(BF)
                to_z(j).start()
            else:
                res[...] = total

        for step in range(8 + LAG):
            if step < 8:
                reduce_block(step, source, psend, grads, to_mate(step).start)
            if 1 <= step < 9:
                stage1(step - 1)
            if step in hooks:
                hooks[step]()
            if step >= LAG and step - LAG not in NEAR_AT:
                stage2(step - LAG)

        for n, j in enumerate(FAR_AT):
            landed(zrecv.at[n], s_ch2.at[j], r_ch2.at[j])
        total = res[...]
        for n in range(5):
            total = total + zrecv[n].astype(F32)
        res[...] = total

        def drain():
            for j in range(8):
                to_mate(j).wait_send()
                if j not in NEAR_AT:
                    for i in range(3):
                        to_y(j, i).wait_send()
                if j < 7:
                    to_z(j).wait_send()

        return drain

    def small(src, dst, ssem, rsem, i):
        return remote(src, dst, ssem.at[i], rsem.at[i], f, gs[YD[i]])

    def small_landed(dst, ssem, rsem):
        for i, d in enumerate(YD):
            ref = dst(gs[(4 - d) % 4])
            remote(ref, ref, ssem.at[i], rsem.at[i], f, gs[1]).wait_recv()

    def h_copy(i):
        return small(hx.at[g], hx.at[g], s_h, r_h, i)

    def c_copy(i):
        return small(cx.at[g], cx.at[g], s_c, r_c, i)

    def w_copy(i):
        return small(w2.at[c, g], w2.at[c, g], s_w, r_w, i)

    def w_mate(i):
        unit = w2.at[c, gs[(4 - YD[i]) % 4]]
        return remote(unit, unit, s_wp.at[i], r_wp.at[i], mate)

    def a_copy(i):
        return small(ax.at[g], ax.at[g], s_a, r_a, i)

    def n1_copy(d):
        return remote(ch.at[zs[d]], cr1.at[d - 1], s_n1.at[d - 1], r_n1.at[d - 1], zpeer[d])

    def n2_copy(d):
        return remote(cs, cr2.at[d - 1], s_n2.at[d - 1], r_n2.at[d - 1], qpeer[d])

    inputs = [
        pltpu.make_async_copy(src, dst, s_in.at[n])
        for n, (src, dst) in enumerate(
            (
                (table_ref, tab.at[c, z, y]),
                (x_ref, xs.at[g]),
                (h_ref, hx.at[g]),
                (cot_ref, cx.at[g]),
                (w_self_ref, w2.at[0, g]),
                (w_neigh_ref, w2.at[1, g]),
                (w_msg_ref, wm),
            )
        )
    ]
    for copy in inputs:
        copy.start()
    keys_v[0] = key_tile(dim_own_ref, dim_slot_ref)
    keys_v[1] = key_tile(ent_own_ref, ent_slot_ref)
    to_keys = [
        pltpu.make_async_copy(keys_v.at[0], keys_dim, s_in.at[7]),
        pltpu.make_async_copy(keys_v.at[1], keys_ent, s_in.at[8]),
    ]
    for copy in to_keys:
        copy.start()
    prepare(dim_own_ref, dim_slot_ref, None, bt_dim, ot_dim)
    prepare(ent_own_ref, ent_slot_ref, b_ent, bt_ent, ot_ent)
    owner_no = lax.broadcasted_iota(jnp.int32, (64, W), 0).astype(F32)
    hits = jnp.zeros((64, W), F32)
    for i in range(ROWS // W):
        orow = jnp.broadcast_to(ent_own_ref[i : i + 1, :].astype(F32), (64, W))
        named = jnp.where(orow == owner_no, 1.0, 0.0).astype(BF)
        hits = hits + jnp.dot(named, b_ent[i * W : (i + 1) * W, :], preferred_element_type=F32)
    ch[...] = hits.reshape(8, 8, W)
    for copy in inputs + to_keys:
        copy.wait()
    pl.semaphore_wait(barrier, len(friends))
    gather_open()
    for n in range(2):
        x_copy(n).start()
    for n in range(2):
        x_copy(n).wait_send()
        x_copy(n + 2).start()
    gather_near()
    for d in range(1, 8):
        n1_copy(d).start()

    def relay_x():
        x_landed(0)
        x_copy(4).start()
        x_landed(1)
        x_copy(5).start()

    def encode():
        for n in range(2, 6):
            x_landed(n)
        for i in range(3):
            h_copy(i).start()
            c_copy(i).start()
            w_copy(i).start()
        feats = jnp.concatenate([xs[b] for b in range(4)], axis=1)
        acc[...] = jnp.dot(feats, wm[...], preferred_element_type=F32)

    def message(rows, found):
        v = acc[rows, :] + found
        s = sigmoid_of(v)
        val[rows, :] = (v * s).astype(BF)
        slope[rows, :] = s * (1.0 + v * (1.0 - s))

    gather_run(keys_dim, message, {0: relay_x, 17: encode})
    gather_drain()

    for d in range(1, 8):
        ref = cr1.at[d - 1]
        landed(ref, s_n1.at[d - 1], r_n1.at[d - 1])
    zsum = ch[z]
    for d in range(1, 8):
        zsum = zsum + cr1[d - 1]
    cs[...] = zsum
    for d in range(1, 8):
        n2_copy(d).start()

    def weights_on():
        small_landed(lambda b: w2.at[c, b], s_w, r_w)
        for i in range(3):
            w_mate(i).start()

    def from_entities():
        small_landed(lambda b: hx.at[b], s_h, r_h)
        small_landed(lambda b: cx.at[b], s_c, r_c)
        for i, d in enumerate(YD):
            ref = w2.at[1 - c, gs[(4 - d) % 4]]
            landed(ref, s_wp.at[i], r_wp.at[i])
        h_full = jnp.concatenate([hx[b] for b in range(4)], axis=1)
        for b in range(4):
            pre[b] = jnp.dot(h_full, w2[0, b], preferred_element_type=F32)

    def divide_by():
        for d in range(1, 8):
            landed(cr2.at[d - 1], s_n2.at[d - 1], r_n2.at[d - 1])
        hsum = cs[...]
        for d in range(1, 8):
            hsum = hsum + cr2[d - 1]
        row_no = lax.broadcasted_iota(jnp.int32, (8, W), 0)
        mine_row = jnp.sum(jnp.where(row_no == q, hsum, 0.0), axis=0, keepdims=True)
        column = jnp.sum(
            jnp.where(eye, jnp.broadcast_to(mine_row, (W, W)), 0.0), axis=1, keepdims=True
        )
        div[...] = jnp.broadcast_to(jnp.maximum(column, 1.0), (W, W))

    drain1 = reduce_all(
        val,
        psend1,
        precv1,
        gsend1,
        grecv1,
        ysend1,
        yrecv1,
        zsend1,
        zrecv1,
        res1,
        False,
        {8: weights_on, 9: divide_by, 10: from_entities},
    )

    ax[g] = (res1[...] / div[...]).astype(BF)
    for i in range(3):
        a_copy(i).start()
    drain1()
    small_landed(lambda b: ax.at[b], s_a, r_a)
    a_full = jnp.concatenate([ax[b] for b in range(4)], axis=1)
    d_agg = jnp.zeros((W, W), F32)
    mine_rows = pl.ds(pl.multiple_of(g * W, W), W)
    for b in range(4):
        v = pre[b] + jnp.dot(a_full, w2[1, b], preferred_element_type=F32)
        pre[b] = v
        s = sigmoid_of(v)
        d_pre = (cx[b].astype(F32) * (s * (1.0 + v * (1.0 - s)))).astype(BF)
        d_agg = d_agg + lax.dot_general(
            d_pre, w2[1, b, mine_rows, :], (((1,), (1,)), ((), ())), preferred_element_type=F32
        )
    tab[c, z, y] = (d_agg / div[...]).astype(BF)
    gather_open()
    v = pre[g]
    s = sigmoid_of(v)
    out_ref[...] = (v * s).astype(BF)
    d_pre = (cx[g].astype(F32) * (s * (1.0 + v * (1.0 - s)))).astype(BF)
    for b in range(4):
        span = slice(b * W, (b + 1) * W)
        gw[1, span, :] = lax.dot_general(
            hx[b], d_pre, (((0,), (0,)), ((), ())), preferred_element_type=F32
        )
        gw[2, span, :] = lax.dot_general(
            ax[b], d_pre, (((0,), (0,)), ((), ())), preferred_element_type=F32
        )

    gather_near()
    def back(rows, found):
        val[rows, :] = (found * slope[rows, :]).astype(BF)

    gather_run(keys_ent, back, {})
    gather_drain()
    for b in range(4):
        gw[0, b * W : (b + 1) * W, :] = lax.dot_general(
            xs[b], val[...], (((0,), (0,)), ((), ())), preferred_element_type=F32
        )
    drain2 = reduce_all(
        val,
        psend2,
        precv2,
        gsend2,
        grecv2,
        ysend2,
        yrecv2,
        zsend2,
        zrecv2,
        res2,
        True,
        {},
    )
    sums_ref[...] = res2[...]

    drain2()
    for n in range(2, 6):
        x_copy(n).wait_send()
    for i in range(3):
        h_copy(i).wait_send()
        c_copy(i).wait_send()
        w_copy(i).wait_send()
        w_mate(i).wait_send()
        a_copy(i).wait_send()
    for d in range(1, 8):
        n1_copy(d).wait_send()
        n2_copy(d).wait_send()


def hand_out(out_in, sums_in, out_ref, gwm_ref, gws_ref, gwn_ref, gdim_ref):
    out_ref[...] = out_in[...]
    gdim_ref[...] = sums_in[0:W]
    gwm_ref[...] = sums_in[W : W + 8]
    gws_ref[...] = sums_in[W + 8 : W + 16]
    gwn_ref[...] = sums_in[W + 16 : W + 24]


def shards(x, dim_owner, dim_slot, fact_owner, fact_slot, table, h, w_msg, w_self, w_neigh, cot):
    tile = (ROWS // W, W)
    vmem = pl.BlockSpec(memory_space=pltpu.VMEM)
    anywhere = pl.BlockSpec(memory_space=pl.ANY)
    dma = pltpu.SemaphoreType.DMA

    def lots(tall, *lead):
        return pltpu.VMEM((*lead, tall, W), BF)

    def stages(tall):
        return [
            lots(tall, 8, NY),
            lots(tall, 8, NY),
            lots(tall, 2, NY),
            lots(tall, 2, NY),
            lots(tall, 6, 3),
            lots(tall, 6, 3),
            lots(tall, 5),
            lots(tall, 5),
        ]

    def sems(*shape):
        return [dma(shape), dma(shape)]

    scratch = [
        lots(ROWS, 4),
        lots(W, 2, NZ, NY),
        pltpu.VMEM((ROWS, W), BF),
        pltpu.VMEM((W, ROWS), BF),
        pltpu.VMEM((W, ROWS), BF),
        pltpu.VMEM((W, ROWS), BF),
        pltpu.VMEM((W, ROWS), BF),
        pltpu.VMEM((ROWS, W), F32),
        pltpu.VMEM((ROWS, W), F32),
        pltpu.VMEM((ROWS, W), BF),
        pltpu.VMEM((8, 8, W), F32),
        pltpu.VMEM((8, W), F32),
        pltpu.VMEM((7, 8, W), F32),
        pltpu.VMEM((7, 8, W), F32),
        lots(W, 4),
        lots(W, 4),
        lots(W, 4),
        lots(512, 2, 4),
        lots(512),
        pltpu.VMEM((4, W, W), F32),
        pltpu.VMEM((3, 512, W), F32),
        pltpu.VMEM((8, NY, EXTRA, W), F32),
        pltpu.VMEM((8, EXTRA, W), F32),
        *stages(W),
        *stages(EXTRA),
        pltpu.VMEM((W, W), F32),
        pltpu.VMEM((EXTRA, W), F32),
        pltpu.VMEM((W, W), F32),
        *sems(9),
        *sems(8, 3),
        *sems(8),
        *sems(9),
        *sems(8, 3),
        *sems(8),
        *sems(6),
        *sems(3),
        *sems(3),
        *sems(3),
        *sems(3),
        *sems(3),
        *sems(7),
        *sems(7),
        dma((9,)),
        pltpu.VMEM((2, ROWS // W, W), jnp.int32),
        pltpu.SMEM((ROWS // W, W), jnp.int32),
        pltpu.SMEM((ROWS // W, W), jnp.int32),
        pltpu.VMEM((2 * NZ * NY * W, W), F32),
    ]
    out, sums = pl.pallas_call(
        kernel,
        out_shape=(
            jax.ShapeDtypeStruct((W, W), BF),
            jax.ShapeDtypeStruct((EXTRA, W), F32),
        ),
        in_specs=[anywhere] + [vmem] * 4 + [anywhere] * 6,
        out_specs=(vmem,) * 2,
        scratch_shapes=scratch,
        compiler_params=pltpu.CompilerParams(
            collective_id=0, has_side_effects=True, vmem_limit_bytes=56 * 1024 * 1024
        ),
    )(
        x,
        dim_owner.reshape(tile),
        dim_slot.reshape(tile),
        fact_owner.reshape(tile),
        fact_slot.reshape(tile),
        table,
        h,
        w_msg,
        w_self,
        w_neigh,
        cot,
    )
    return pl.pallas_call(
        hand_out,
        out_shape=(
            jax.ShapeDtypeStruct((W, W), BF),
            jax.ShapeDtypeStruct((8, W), F32),
            jax.ShapeDtypeStruct((8, W), F32),
            jax.ShapeDtypeStruct((8, W), F32),
            jax.ShapeDtypeStruct((W, W), F32),
        ),
        in_specs=[vmem] * 2,
        out_specs=(vmem,) * 5,
    )(out, sums)


def solution(mesh):
    placed = (
        P("fact", "feat"),
        P("fact", None),
        P("fact"),
        P("fact", None),
        P("fact"),
        P("fact", "feat"),
        P("fact", "feat"),
        P(None, "feat"),
        P(None, "feat"),
        P(None, "feat"),
        P("fact", "feat"),
    )
    return jax.shard_map(
        shards,
        mesh=mesh,
        in_specs=placed,
        out_specs=(P("fact", "feat"),) * 5,
        check_vma=False,
    )
```

```python
import jax
import jax.numpy as jnp
from jax import lax
from jax.experimental import pallas as pl
from jax.experimental.pallas import tpu as pltpu
from jax.sharding import PartitionSpec as P

MESH = pl.DeviceIdType.MESH
BF = jnp.bfloat16
F32 = jnp.float32

NZ, NY = 8, 4
EVENTS = (0, -2, 2, -3, 3, 4, -1, 1)
FAR = 6
TARGETS = (4, -3, 1, -1, 3, -2, 2, 0)
NEAR_AT = (2, 3)
FAR_AT = (0, 1, 4, 5, 6)
YD = (2, 1, 3)
ROWS = 1024
TILE = 256
W = 128
EXTRA = 160
LAG = 5
SPLIT = (0, 1, 5, 6, 7)


def sigmoid_of(v):
    return 1.0 / (1.0 + jnp.exp(-v))


def kernel(
    x_ref,
    dim_own_ref,
    dim_slot_ref,
    ent_own_ref,
    ent_slot_ref,
    table_ref,
    h_ref,
    w_msg_ref,
    w_self_ref,
    w_neigh_ref,
    cot_ref,
    out_ref,
    sums_ref,
    xs,
    tab,
    b_ent,
    bt_dim,
    bt_ent,
    ot_dim,
    ot_ent,
    acc,
    slope,
    val,
    ch,
    cs,
    cr1,
    cr2,
    hx,
    cx,
    ax,
    w2,
    wm,
    pre,
    gw,
    pown,
    yown,
    psend1,
    precv1,
    gsend1,
    grecv1,
    ysend1,
    yrecv1,
    zsend1,
    zrecv1,
    psend2,
    precv2,
    gsend2,
    grecv2,
    ysend2,
    yrecv2,
    zsend2,
    zrecv2,
    res1,
    res2,
    div,
    s_ch,
    r_ch,
    s_y,
    r_y,
    s_p,
    r_p,
    s_ch2,
    r_ch2,
    s_y2,
    r_y2,
    s_p2,
    r_p2,
    s_x,
    r_x,
    s_h,
    r_h,
    s_c,
    r_c,
    s_w,
    r_w,
    s_wp,
    r_wp,
    s_a,
    r_a,
    s_n1,
    r_n1,
    s_n2,
    r_n2,
    s_in,
    keys_v,
    keys_dim,
    keys_ent,
    wide,
):
    f = lax.axis_index("fact")
    g = lax.axis_index("feat")
    z, y, c = f // 8, lax.rem(f // 2, 4), lax.rem(f, 2)
    q = lax.rem(f, 8)

    def at(zz, yy, cc):
        return (zz * 4 + yy) * 2 + cc

    zs = [lax.rem(z + d, NZ) for d in range(NZ)]
    ys = [lax.rem(y + d, NY) for d in range(NY)]
    gs = [lax.rem(g + d, 4) for d in range(4)]
    right, left, mate = at(zs[1], y, c), at(zs[7], y, c), at(z, y, 1 - c)
    zpeer = [at(zs[d], y, c) for d in range(NZ)]
    ypeer = [at(z, ys[d], c) for d in YD]
    qpeer = [z * 8 + lax.rem(q + d, 8) for d in range(8)]

    def remote(src, dst, ssem, rsem, to_f, to_g=None):
        return pltpu.make_async_remote_copy(
            src_ref=src,
            dst_ref=dst,
            send_sem=ssem,
            recv_sem=rsem,
            device_id=(to_f, g if to_g is None else to_g),
            device_id_type=MESH,
        )

    barrier = pltpu.get_barrier_semaphore()
    friends = [(p, g) for p in zpeer[1:]] + [(p, g) for p in qpeer[1:]] + [(f, p) for p in gs[1:]]
    for friend in friends:
        pl.semaphore_signal(barrier, inc=1, device_id=friend, device_id_type=MESH)

    half = [pl.ds(0, ROWS // 2), pl.ds(ROWS // 2, ROWS // 2)]

    def x_copy(n):
        if n < 4:
            to, part = ((1, 0), (3, 1), (1, 1), (3, 0))[n]
            src = xs.at[g, half[part]]
            dst = src
        elif n == 4:
            to, src = 1, xs.at[gs[3], half[0]]
            dst = src
        else:
            to, src = 3, xs.at[gs[1], half[1]]
            dst = src
        return remote(src, dst, s_x.at[n], r_x.at[n], f, gs[to])

    def x_landed(n):
        block, part = ((3, 0), (1, 1), (3, 1), (1, 0), (2, 0), (2, 1))[n]
        dst = xs.at[gs[block], half[part]]
        remote(dst, dst, s_x.at[n], r_x.at[n], f, gs[1]).wait_recv()

    def unit(k):
        return tab.at[c, zs[EVENTS[k] % NZ], y]

    def group(k):
        return tab.at[c, zs[EVENTS[k] % NZ]]

    def z_send(k):
        piece = unit(0) if k < FAR else group(0)
        return remote(piece, piece, s_ch.at[k], r_ch.at[k], zpeer[-EVENTS[k] % NZ])

    def y_send(k, i):
        return remote(unit(k), unit(k), s_y.at[k, i], r_y.at[k, i], ypeer[i])

    def p_send(k):
        return remote(group(k), group(k), s_p.at[k], r_p.at[k], mate)

    def landed(dst, ssem, rsem):
        remote(dst, dst, ssem, rsem, mate).wait_recv()

    def gather_open():
        for k in range(1, FAR):
            z_send(k).start()
        for i in range(3):
            y_send(0, i).start()

    def gather_near():
        gather_join(0)
        for k in (6, 7):
            z_send(k).start()

    def gather_spread(k):
        landed(unit(k), s_ch.at[k], r_ch.at[k])
        for i in range(3):
            y_send(k, i).start()

    def gather_join(k):
        zk = zs[EVENTS[k] % NZ]
        if k < FAR:
            for i, d in enumerate(YD):
                landed(tab.at[c, zk, ys[(NY - d) % NY]], s_y.at[k, i], r_y.at[k, i])
        else:
            landed(group(k), s_ch.at[k], r_ch.at[k])
        p_send(k).start()

    def gather_drain():
        for k in range(8):
            if k > 0:
                z_send(k).wait_send()
            if k < FAR:
                for i in range(3):
                    y_send(k, i).wait_send()
            p_send(k).wait_send()

    def gather_run(keys, sink, hooks):
        def use(k):
            zk = zs[EVENTS[k] % NZ]
            landed(tab.at[1 - c, zk], s_p.at[k], r_p.at[k])
            for parity in (0, 1):
                first = parity * NZ * NY * W + zk * (NY * W)
                rows = pl.ds(pl.multiple_of(first, NY * W), NY * W)
                wide[rows, :] = tab[parity, zk].reshape(NY * W, W).astype(F32)

        plan = (
            (gather_spread, 1),
            (gather_spread, 2),
            (use, 0),
            (gather_spread, 3),
            (gather_spread, 4),
            (gather_spread, 5),
            (gather_join, 1),
            (gather_join, 2),
            (gather_join, 6),
            (gather_join, 7),
            (gather_join, 3),
            (gather_join, 4),
            (use, 1),
            (use, 2),
            (use, 6),
            (use, 7),
            (gather_join, 5),
            (use, 3),
            (use, 4),
            (use, 5),
        )
        for n, (stage, k) in enumerate(plan):
            if n in hooks:
                hooks[n]()
            stage(k)

        def some(t, carry):
            i, first = t // 4, lax.rem(t, 4) * 32
            found = [wide[pl.ds(keys[i, first + j], 1), :] for j in range(32)]
            sink(pl.ds(pl.multiple_of(t * 32, 32), 32), jnp.concatenate(found, axis=0))
            return carry

        lax.fori_loop(0, ROWS // 32, some, 0)

    def key_tile(own_ref, slot_ref):
        owns = own_ref[...]
        return lax.rem(owns, 2) * (NZ * NY * W) + (owns // 2) * W + slot_ref[...]

    def lane_rows(index_ref, i):
        return jnp.broadcast_to(index_ref[i : i + 1, :].astype(F32), (W, W))

    sub = lax.broadcasted_iota(jnp.int32, (W, W), 0)
    lane = lax.broadcasted_iota(jnp.int32, (W, W), 1)
    eye = sub == lane
    subf, lanef = sub.astype(F32), lane.astype(F32)
    ones_w = jnp.ones((W, W), BF)

    def prepare(own_ref, slot_ref, slots, slots_t, owners_t):
        for i in range(ROWS // W):
            span = slice(i * W, (i + 1) * W)
            srow = lane_rows(slot_ref, i)
            slots_t[:, span] = jnp.where(srow == subf, 1.0, 0.0).astype(BF)
            if slots is not None:
                scol = jnp.dot(
                    jnp.where(eye, srow, 0.0).astype(BF), ones_w, preferred_element_type=F32
                )
                slots[span, :] = jnp.where(scol == lanef, 1.0, 0.0).astype(BF)
            oint = own_ref[i : i + 1, :]
            flipped = oint + c * (1 - 2 * lax.rem(oint, 2))
            owners_t[:, span] = jnp.broadcast_to(flipped.astype(F32), (W, W)).astype(BF)

    def reduce_block(j, source, psend, grads, send):
        tz = zs[TARGETS[j] % NZ]
        owners_t, slots_t = (ot_dim, bt_dim) if grads else (ot_ent, bt_ent)

        base = (tz * 8).astype(F32)
        rel = owners_t[...] - jnp.full((W, ROWS), base, F32).astype(BF)
        ones = slots_t[...]
        zero = jnp.zeros_like(ones)
        def product(sides):
            lhs = jnp.concatenate(
                [
                    jnp.where(rel == jnp.asarray(yy * 2 + side, BF), ones, zero)
                    for side in sides
                    for yy in range(NY)
                ],
                axis=0,
            )
            return jnp.dot(lhs, source[...], preferred_element_type=F32)

        def blocks(got, first):
            return [got[(first + yy) * W : (first + yy + 1) * W] for yy in range(NY)]

        if j in SPLIT:
            theirs = blocks(product((1,)), 0)
        else:
            got = product((1, 0))
            theirs, ours = blocks(got, 0), blocks(got, NY)
        for yy in range(NY):
            psend[j, yy, 0:W] = theirs[yy].astype(BF)
        if grads:
            blank = jnp.zeros((8, W), F32)
            for yy in range(NY):
                first = tz * 8 + yy * 2
                mine = pl.ds(pl.multiple_of((first + c) * 8, 8), 8)
                other = pl.ds(pl.multiple_of((first + 1 - c) * 8, 8), 8)
                for n in range(3):
                    pown[j, yy, W + 8 * n : W + 8 * n + 8] = gw[n, mine, :]
                pown[j, yy, W + 24 : W + 32] = blank
                psend[j, yy, W : W + 16] = jnp.concatenate(
                    [gw[0, other, :], gw[1, other, :]], axis=0
                ).astype(BF)
                psend[j, yy, W + 16 : W + 32] = jnp.concatenate(
                    [gw[2, other, :], blank], axis=0
                ).astype(BF)
        send()
        if j in SPLIT:
            ours = blocks(product((0,)), 0)
        for yy in range(NY):
            pown[j, yy, 0:W] = ours[yy]

    def reduce_all(
        source, psend, precv, gsend, grecv, ysend, yrecv, zsend, zrecv, res, grads, hooks
    ):
        tall = pl.ds(0, EXTRA if grads else W)

        def to_mate(j):
            return remote(psend.at[j], precv.at[j], s_p2.at[j], r_p2.at[j], mate)

        def slot(j):
            return 5 if j == 7 else FAR_AT.index(j)

        def to_y(j, i):
            n = slot(j)
            return remote(ysend.at[n, i], yrecv.at[n, i], s_y2.at[n, i], r_y2.at[n, i], ypeer[i])

        def to_z(j):
            to = zpeer[TARGETS[j] % NZ]
            if j in NEAR_AT:
                n = NEAR_AT.index(j)
                return remote(gsend.at[n], grecv.at[n], s_ch2.at[j], r_ch2.at[j], to)
            n = slot(j)
            return remote(zsend.at[n], zrecv.at[n], s_ch2.at[j], r_ch2.at[j], to)

        def stage1(j):
            landed(precv.at[j], s_p2.at[j], r_p2.at[j])
            if j in NEAR_AT:
                gsend[NEAR_AT.index(j)] = (pown[j, :, tall] + precv[j].astype(F32)).astype(BF)
                to_z(j).start()
                return
            if j == 7:
                for n in range(2):
                    landed(grecv.at[n], s_ch2.at[NEAR_AT[n]], r_ch2.at[NEAR_AT[n]])

            def block(yy):
                got = pown[j, yy, tall] + precv[j, yy].astype(F32)
                if j == 7:
                    for n in range(2):
                        got = got + grecv[n, yy].astype(F32)
                return got

            for i, d in enumerate(YD):
                ysend[slot(j), i] = block(ys[d]).astype(BF)
                to_y(j, i).start()
            yown[j, tall] = block(y)

        def stage2(j):
            for i in range(3):
                n = slot(j)
                landed(yrecv.at[n, i], s_y2.at[n, i], r_y2.at[n, i])
            total = yown[j, tall]
            for i in range(3):
                total = total + yrecv[slot(j), i].astype(F32)
            if j < 7:
                zsend[slot(j)] = total.astype(BF)
                to_z(j).start()
            else:
                res[...] = total

        for step in range(8 + LAG):
            if step < 8:
                reduce_block(step, source, psend, grads, to_mate(step).start)
            if 1 <= step < 9:
                stage1(step - 1)
            if step in hooks:
                hooks[step]()
            if step >= LAG and step - LAG not in NEAR_AT:
                stage2(step - LAG)

        for n, j in enumerate(FAR_AT):
            landed(zrecv.at[n], s_ch2.at[j], r_ch2.at[j])
        total = res[...]
        for n in range(5):
            total = total + zrecv[n].astype(F32)
        res[...] = total

        def drain():
            for j in range(8):
                to_mate(j).wait_send()
                if j not in NEAR_AT:
                    for i in range(3):
                        to_y(j, i).wait_send()
                if j < 7:
                    to_z(j).wait_send()

        return drain

    def small(src, dst, ssem, rsem, i):
        return remote(src, dst, ssem.at[i], rsem.at[i], f, gs[YD[i]])

    def small_landed(dst, ssem, rsem):
        for i, d in enumerate(YD):
            ref = dst(gs[(4 - d) % 4])
            remote(ref, ref, ssem.at[i], rsem.at[i], f, gs[1]).wait_recv()

    def h_copy(i):
        return small(hx.at[g], hx.at[g], s_h, r_h, i)

    def c_copy(i):
        return small(cx.at[g], cx.at[g], s_c, r_c, i)

    def w_copy(i):
        return small(w2.at[c, g], w2.at[c, g], s_w, r_w, i)

    def w_mate(i):
        unit = w2.at[c, gs[(4 - YD[i]) % 4]]
        return remote(unit, unit, s_wp.at[i], r_wp.at[i], mate)

    def a_copy(i):
        return small(ax.at[g], ax.at[g], s_a, r_a, i)

    def n1_copy(d):
        return remote(ch.at[zs[d]], cr1.at[d - 1], s_n1.at[d - 1], r_n1.at[d - 1], zpeer[d])

    def n2_copy(d):
        return remote(cs, cr2.at[d - 1], s_n2.at[d - 1], r_n2.at[d - 1], qpeer[d])

    inputs = [
        pltpu.make_async_copy(src, dst, s_in.at[n])
        for n, (src, dst) in enumerate(
            (
                (table_ref, tab.at[c, z, y]),
                (x_ref, xs.at[g]),
                (h_ref, hx.at[g]),
                (cot_ref, cx.at[g]),
                (w_self_ref, w2.at[0, g]),
                (w_neigh_ref, w2.at[1, g]),
                (w_msg_ref, wm),
            )
        )
    ]
    for copy in inputs:
        copy.start()
    keys_v[0] = key_tile(dim_own_ref, dim_slot_ref)
    keys_v[1] = key_tile(ent_own_ref, ent_slot_ref)
    to_keys = [
        pltpu.make_async_copy(keys_v.at[0], keys_dim, s_in.at[7]),
        pltpu.make_async_copy(keys_v.at[1], keys_ent, s_in.at[8]),
    ]
    for copy in to_keys:
        copy.start()
    prepare(dim_own_ref, dim_slot_ref, None, bt_dim, ot_dim)
    prepare(ent_own_ref, ent_slot_ref, b_ent, bt_ent, ot_ent)
    owner_no = lax.broadcasted_iota(jnp.int32, (64, W), 0).astype(F32)
    hits = jnp.zeros((64, W), F32)
    for i in range(ROWS // W):
        orow = jnp.broadcast_to(ent_own_ref[i : i + 1, :].astype(F32), (64, W))
        named = jnp.where(orow == owner_no, 1.0, 0.0).astype(BF)
        hits = hits + jnp.dot(named, b_ent[i * W : (i + 1) * W, :], preferred_element_type=F32)
    ch[...] = hits.reshape(8, 8, W)
    for copy in inputs + to_keys:
        copy.wait()
    pl.semaphore_wait(barrier, len(friends))
    gather_open()
    for n in range(2):
        x_copy(n).start()
    for n in range(2):
        x_copy(n).wait_send()
        x_copy(n + 2).start()
    gather_near()
    for d in range(1, 8):
        n1_copy(d).start()

    def relay_x():
        x_landed(0)
        x_copy(4).start()
        x_landed(1)
        x_copy(5).start()

    def encode():
        for n in range(2, 6):
            x_landed(n)
        for i in range(3):
            h_copy(i).start()
            c_copy(i).start()
            w_copy(i).start()
        feats = jnp.concatenate([xs[b] for b in range(4)], axis=1)
        acc[...] = jnp.dot(feats, wm[...], preferred_element_type=F32)

    def message(rows, found):
        v = acc[rows, :] + found
        s = sigmoid_of(v)
        val[rows, :] = (v * s).astype(BF)
        slope[rows, :] = s * (1.0 + v * (1.0 - s))

    gather_run(keys_dim, message, {0: relay_x, 17: encode})
    gather_drain()

    for d in range(1, 8):
        ref = cr1.at[d - 1]
        landed(ref, s_n1.at[d - 1], r_n1.at[d - 1])
    zsum = ch[z]
    for d in range(1, 8):
        zsum = zsum + cr1[d - 1]
    cs[...] = zsum
    for d in range(1, 8):
        n2_copy(d).start()

    def weights_on():
        small_landed(lambda b: w2.at[c, b], s_w, r_w)
        for i in range(3):
            w_mate(i).start()

    def from_entities():
        small_landed(lambda b: hx.at[b], s_h, r_h)
        small_landed(lambda b: cx.at[b], s_c, r_c)
        for i, d in enumerate(YD):
            ref = w2.at[1 - c, gs[(4 - d) % 4]]
            landed(ref, s_wp.at[i], r_wp.at[i])
        h_full = jnp.concatenate([hx[b] for b in range(4)], axis=1)
        for b in range(4):
            pre[b] = jnp.dot(h_full, w2[0, b], preferred_element_type=F32)

    def divide_by():
        for d in range(1, 8):
            landed(cr2.at[d - 1], s_n2.at[d - 1], r_n2.at[d - 1])
        hsum = cs[...]
        for d in range(1, 8):
            hsum = hsum + cr2[d - 1]
        row_no = lax.broadcasted_iota(jnp.int32, (8, W), 0)
        mine_row = jnp.sum(jnp.where(row_no == q, hsum, 0.0), axis=0, keepdims=True)
        column = jnp.sum(
            jnp.where(eye, jnp.broadcast_to(mine_row, (W, W)), 0.0), axis=1, keepdims=True
        )
        div[...] = jnp.broadcast_to(jnp.maximum(column, 1.0), (W, W))

    drain1 = reduce_all(
        val,
        psend1,
        precv1,
        gsend1,
        grecv1,
        ysend1,
        yrecv1,
        zsend1,
        zrecv1,
        res1,
        False,
        {8: weights_on, 9: divide_by, 10: from_entities},
    )

    ax[g] = (res1[...] / div[...]).astype(BF)
    for i in range(3):
        a_copy(i).start()
    drain1()
    small_landed(lambda b: ax.at[b], s_a, r_a)
    a_full = jnp.concatenate([ax[b] for b in range(4)], axis=1)
    d_agg = jnp.zeros((W, W), F32)
    mine_rows = pl.ds(pl.multiple_of(g * W, W), W)
    for b in range(4):
        v = pre[b] + jnp.dot(a_full, w2[1, b], preferred_element_type=F32)
        pre[b] = v
        s = sigmoid_of(v)
        d_pre = (cx[b].astype(F32) * (s * (1.0 + v * (1.0 - s)))).astype(BF)
        d_agg = d_agg + lax.dot_general(
            d_pre, w2[1, b, mine_rows, :], (((1,), (1,)), ((), ())), preferred_element_type=F32
        )
    tab[c, z, y] = (d_agg / div[...]).astype(BF)
    gather_open()
    v = pre[g]
    s = sigmoid_of(v)
    out_ref[...] = (v * s).astype(BF)
    d_pre = (cx[g].astype(F32) * (s * (1.0 + v * (1.0 - s)))).astype(BF)
    for b in range(4):
        span = slice(b * W, (b + 1) * W)
        gw[1, span, :] = lax.dot_general(
            hx[b], d_pre, (((0,), (0,)), ((), ())), preferred_element_type=F32
        )
        gw[2, span, :] = lax.dot_general(
            ax[b], d_pre, (((0,), (0,)), ((), ())), preferred_element_type=F32
        )

    gather_near()
    def back(rows, found):
        val[rows, :] = (found * slope[rows, :]).astype(BF)

    gather_run(keys_ent, back, {})
    gather_drain()
    for b in range(4):
        gw[0, b * W : (b + 1) * W, :] = lax.dot_general(
            xs[b], val[...], (((0,), (0,)), ((), ())), preferred_element_type=F32
        )
    drain2 = reduce_all(
        val,
        psend2,
        precv2,
        gsend2,
        grecv2,
        ysend2,
        yrecv2,
        zsend2,
        zrecv2,
        res2,
        True,
        {},
    )
    sums_ref[...] = res2[...]

    drain2()
    for n in range(2, 6):
        x_copy(n).wait_send()
    for i in range(3):
        h_copy(i).wait_send()
        c_copy(i).wait_send()
        w_copy(i).wait_send()
        w_mate(i).wait_send()
        a_copy(i).wait_send()
    for d in range(1, 8):
        n1_copy(d).wait_send()
        n2_copy(d).wait_send()


def hand_out(out_in, sums_in, out_ref, gwm_ref, gws_ref, gwn_ref, gdim_ref):
    out_ref[...] = out_in[...]
    gdim_ref[...] = sums_in[0:W]
    gwm_ref[...] = sums_in[W : W + 8]
    gws_ref[...] = sums_in[W + 8 : W + 16]
    gwn_ref[...] = sums_in[W + 16 : W + 24]


def shards(x, dim_owner, dim_slot, fact_owner, fact_slot, table, h, w_msg, w_self, w_neigh, cot):
    tile = (ROWS // W, W)
    vmem = pl.BlockSpec(memory_space=pltpu.VMEM)
    anywhere = pl.BlockSpec(memory_space=pl.ANY)
    dma = pltpu.SemaphoreType.DMA

    def lots(tall, *lead):
        return pltpu.VMEM((*lead, tall, W), BF)

    def stages(tall):
        return [
            lots(tall, 8, NY),
            lots(tall, 8, NY),
            lots(tall, 2, NY),
            lots(tall, 2, NY),
            lots(tall, 6, 3),
            lots(tall, 6, 3),
            lots(tall, 5),
            lots(tall, 5),
        ]

    def sems(*shape):
        return [dma(shape), dma(shape)]

    scratch = [
        lots(ROWS, 4),
        lots(W, 2, NZ, NY),
        pltpu.VMEM((ROWS, W), BF),
        pltpu.VMEM((W, ROWS), BF),
        pltpu.VMEM((W, ROWS), BF),
        pltpu.VMEM((W, ROWS), BF),
        pltpu.VMEM((W, ROWS), BF),
        pltpu.VMEM((ROWS, W), F32),
        pltpu.VMEM((ROWS, W), F32),
        pltpu.VMEM((ROWS, W), BF),
        pltpu.VMEM((8, 8, W), F32),
        pltpu.VMEM((8, W), F32),
        pltpu.VMEM((7, 8, W), F32),
        pltpu.VMEM((7, 8, W), F32),
        lots(W, 4),
        lots(W, 4),
        lots(W, 4),
        lots(512, 2, 4),
        lots(512),
        pltpu.VMEM((4, W, W), F32),
        pltpu.VMEM((3, 512, W), F32),
        pltpu.VMEM((8, NY, EXTRA, W), F32),
        pltpu.VMEM((8, EXTRA, W), F32),
        *stages(W),
        *stages(EXTRA),
        pltpu.VMEM((W, W), F32),
        pltpu.VMEM((EXTRA, W), F32),
        pltpu.VMEM((W, W), F32),
        *sems(9),
        *sems(8, 3),
        *sems(8),
        *sems(9),
        *sems(8, 3),
        *sems(8),
        *sems(6),
        *sems(3),
        *sems(3),
        *sems(3),
        *sems(3),
        *sems(3),
        *sems(7),
        *sems(7),
        dma((9,)),
        pltpu.VMEM((2, ROWS // W, W), jnp.int32),
        pltpu.SMEM((ROWS // W, W), jnp.int32),
        pltpu.SMEM((ROWS // W, W), jnp.int32),
        pltpu.VMEM((2 * NZ * NY * W, W), F32),
    ]
    out, sums = pl.pallas_call(
        kernel,
        out_shape=(
            jax.ShapeDtypeStruct((W, W), BF),
            jax.ShapeDtypeStruct((EXTRA, W), F32),
        ),
        in_specs=[anywhere] + [vmem] * 4 + [anywhere] * 6,
        out_specs=(vmem,) * 2,
        scratch_shapes=scratch,
        compiler_params=pltpu.CompilerParams(
            collective_id=0, has_side_effects=True, vmem_limit_bytes=56 * 1024 * 1024
        ),
    )(
        x,
        dim_owner.reshape(tile),
        dim_slot.reshape(tile),
        fact_owner.reshape(tile),
        fact_slot.reshape(tile),
        table,
        h,
        w_msg,
        w_self,
        w_neigh,
        cot,
    )
    return pl.pallas_call(
        hand_out,
        out_shape=(
            jax.ShapeDtypeStruct((W, W), BF),
            jax.ShapeDtypeStruct((8, W), F32),
            jax.ShapeDtypeStruct((8, W), F32),
            jax.ShapeDtypeStruct((8, W), F32),
            jax.ShapeDtypeStruct((W, W), F32),
        ),
        in_specs=[vmem] * 2,
        out_specs=(vmem,) * 5,
    )(out, sums)


def solution(mesh):
    placed = (
        P("fact", "feat"),
        P("fact", None),
        P("fact"),
        P("fact", None),
        P("fact"),
        P("fact", "feat"),
        P("fact", "feat"),
        P(None, "feat"),
        P(None, "feat"),
        P(None, "feat"),
        P("fact", "feat"),
    )
    return jax.shard_map(
        shards,
        mesh=mesh,
        in_specs=placed,
        out_specs=(P("fact", "feat"),) * 5,
        check_vma=False,
    )
```
